512 devices in a mesh: grp: 16 (over x, y_hi), ctx: 32 (over y_lo, z, core).
Axes of the slice: x: 4, y: 8 (y_hi: 4, y_lo: 2; y = y_hi * 2 + y_lo), z: 8, core: 2. Of those that a mesh axis runs over, the one named last changes fastest.
Arguments:
- query_raw: bfloat16 [131072, 256], P(('grp', 'ctx')), may hold values from -6 to 6
- key_raw: bfloat16 [131072, 256], P(('grp', 'ctx')), may hold values from -6 to 6
- values: bfloat16 [131072, 256], P(('grp', 'ctx')), may hold values from -6 to 6
- band_reach: int32 [1024], P(('grp', 'ctx')), may hold values from 1 to 2, as said below
- partners: int32 [1024, 4], P(('grp', 'ctx')), may hold values from 0 to 1023, as said below
- gain_query: float32 [2, 128], replicated, may hold values from 0.5 to 2
- gain_key: float32 [2, 128], replicated, may hold values from 0.5 to 2
- cotangent: bfloat16 [131072, 256], P(('grp', 'ctx')), may hold values from -6 to 6
Outputs:
- output: bfloat16 [131072, 256], P(('grp', 'ctx'))
- grad_query: bfloat16 [131072, 256], P(('grp', 'ctx'))
- grad_key: bfloat16 [131072, 256], P(('grp', 'ctx'))
- grad_value: bfloat16 [131072, 256], P(('grp', 'ctx'))
The draws below stay inside these ranges and needn't reach their ends.
Inputs may be any that keep to these rules, and one draw needn't show every extreme that they name: `band_reach`: some query block has reach 2. partners[b, l] is a block of the device whose index is (b // 2) xor (512 // 2**(l+1)).
All inputs are finite; a program needn't handle non-finite values.
Results may differ from the reference program's by a relative error of at most 0.0099.
Values may be sent and summed in bfloat16 or wider, within the bound.
No kernel may reach another device: no remote copies, remote signals or barrier semaphores. Data moves between devices by JAX's collectives and lax.ppermute only.
A program may use at most 64 MiB of HBM per device.

```python
import math
import jax
import jax.numpy as jnp
from jax import lax

HEADS = 2
HEAD_DIM = 128
BLOCK = 128
BAND = 2
LEVELS = 4
SHARDS = 512
TOKENS = 131072
BLOCKS_DEV = 2
BLOCKS = 1024


def draw_band_reach(key, part):
    reach = jax.random.randint(key, (BLOCKS,), 1, BAND + 1)
    places = jnp.arange(BLOCKS)
    reach = jnp.where(places == 0, 1, reach)
    reach = jnp.where(places == 1, BAND, reach)
    return reach.astype(jnp.int32)


def draw_partners(key, part):
    block_ids = jnp.arange(BLOCKS, dtype=jnp.int32)[:, None]
    level_ids = jnp.arange(LEVELS, dtype=jnp.int32)[None, :]
    distance = jnp.right_shift(jnp.int32(SHARDS), level_ids + 1)
    owner = block_ids // BLOCKS_DEV
    partner_device = jnp.bitwise_xor(owner, distance)
    picked = jax.random.randint(key, (BLOCKS, LEVELS), 0, BLOCKS_DEV)
    picked = jnp.where(owner == SHARDS // 2 - 1, BLOCKS_DEV - 1, picked)
    picked = jnp.where(owner == SHARDS // 2, 0, picked)
    return (partner_device * BLOCKS_DEV + picked).astype(jnp.int32)


def steps_of(rng, extent, cuts, smallest, high):
    def one(axis_at, parts):
        draws = jax.random.uniform(jax.random.fold_in(jax.random.fold_in(rng, 6), axis_at), (parts,), jnp.float32, smallest / len(cuts), high / len(cuts))
        return jnp.repeat(jnp.exp(draws), extent[axis_at] // parts).reshape((-1,) + (1,) * (len(extent) - axis_at - 1))

    level = one(*cuts[0])
    for cut in cuts[1:]:
        level = level * one(*cut)
    return level


def bell_draw(rng, dims, width, most, shards=(), kind=jnp.bfloat16):
    array = width * jax.random.normal(rng, dims, jnp.float32)
    if shards:
        array = array * steps_of(rng, dims, shards, -0.22, 0.18)
    return jnp.clip(array, -most, most).astype(kind)


def setup_inputs(seed: int = 0) -> dict:
    keys = jax.random.split(jax.random.key(seed), 9)
    return {
        "query_raw": bell_draw(keys[0], (TOKENS, HEADS * HEAD_DIM), 1.0, 6.0, ((0, 512),)),
        "key_raw": bell_draw(keys[1], (TOKENS, HEADS * HEAD_DIM), 1.0, 6.0, ((0, 512),)),
        "values": bell_draw(keys[2], (TOKENS, HEADS * HEAD_DIM), 1.0, 6.0, ((0, 512),)),
        "band_reach": draw_band_reach(jax.random.fold_in(keys[8], 71), 0),
        "partners": draw_partners(jax.random.fold_in(keys[8], 71), 0),
        "gain_query": jnp.clip(jnp.exp(jax.random.uniform(keys[5], (HEADS, HEAD_DIM), jnp.float32, math.log(0.5), math.log(2.0))), 0.5, 2.0),
        "gain_key": jnp.clip(jnp.exp(jax.random.uniform(keys[6], (HEADS, HEAD_DIM), jnp.float32, math.log(0.5), math.log(2.0))), 0.5, 2.0),
        "cotangent": bell_draw(keys[7], (TOKENS, HEADS * HEAD_DIM), 1.0, 6.0, ((0, 512),)),
    }


epsilon = 1e-05

def layer_norm(inputs, gain_row):
    average = lax.optimization_barrier(jnp.mean(inputs, axis=-1, keepdims=True))
    centred = inputs - average
    inverse = lax.rsqrt(lax.optimization_barrier(jnp.mean(centred * centred, axis=-1, keepdims=True)) + epsilon)
    normed = centred * inverse
    return (normed, inverse, normed * gain_row)

def norm_back(upstream, normed, inverse, gain_row):
    scaled = upstream * gain_row
    first = lax.optimization_barrier(jnp.mean(scaled, axis=-1, keepdims=True))
    second = lax.optimization_barrier(jnp.mean(scaled * normed, axis=-1, keepdims=True))
    return (scaled - first - normed * second) * inverse

def reference(query_raw, key_raw, values, band_reach, partners, gain_query, gain_key, cotangent):
    tokens, row_width = query_raw.shape
    head_dim = row_width // HEADS
    block_count = tokens // BLOCK
    score_scale = head_dim ** (-0.5)
    q_normed, q_inverse, q_scaled = layer_norm(query_raw.astype(jnp.float32).reshape(tokens, HEADS, head_dim), gain_query)
    k_normed, k_inverse, k_scaled = layer_norm(key_raw.astype(jnp.float32).reshape(tokens, HEADS, head_dim), gain_key)
    query_low = q_scaled.astype(jnp.bfloat16).reshape(block_count, BLOCK, HEADS, head_dim)
    key_low = k_scaled.astype(jnp.bfloat16).reshape(block_count, BLOCK, HEADS, head_dim)
    value_blocks = values.reshape(block_count, BLOCK, HEADS, head_dim)
    grad_blocks = cotangent.reshape(block_count, BLOCK, HEADS, head_dim)
    offsets = jnp.arange(2 * BAND + 1, dtype=jnp.int32) - BAND

    def block_step(totals, block_index):
        key_acc, value_acc = totals
        target = block_index + offsets
        band_ok = (jnp.abs(offsets) <= band_reach[block_index]) & (target >= 0) & (target < block_count)
        chosen = jnp.concatenate((jnp.clip(target, 0, block_count - 1).astype(jnp.int32), partners[block_index].astype(jnp.int32)))
        usable = jnp.concatenate((band_ok, jnp.ones((LEVELS,), dtype=jnp.bool_)))
        key_set = key_low[chosen].astype(jnp.float32)
        value_set = value_blocks[chosen].astype(jnp.float32)
        query_block = query_low[block_index].astype(jnp.float32)
        grad_block = grad_blocks[block_index].astype(jnp.float32)
        scores = jnp.einsum('qhd,jkhd->hqjk', query_block, key_set) * score_scale
        allowed = usable[None, None, :, None]
        row_total = lax.optimization_barrier(jnp.sum(jnp.where(allowed, jnp.exp(scores), 0.0), axis=(2, 3)))
        log_total = jnp.log(row_total)
        probability = jnp.where(allowed, jnp.exp(scores - log_total[:, :, None, None]), 0.0)
        attention_weight = lax.optimization_barrier(probability.astype(jnp.bfloat16)).astype(jnp.float32)
        output = jnp.einsum('hqjk,jkhd->qhd', attention_weight, value_set).astype(jnp.bfloat16)
        row_delta = lax.optimization_barrier(jnp.sum(grad_block * output.astype(jnp.float32), axis=-1))
        grad_prob = jnp.einsum('qhd,jkhd->hqjk', grad_block, value_set)
        score_gradient = probability * (grad_prob - jnp.transpose(row_delta)[:, :, None, None])
        score_gradient = lax.optimization_barrier(score_gradient.astype(jnp.bfloat16)).astype(jnp.float32)
        grad_qnorm = jnp.einsum('hqjk,jkhd->qhd', score_gradient, key_set) * score_scale
        key_terms = jnp.einsum('hqjk,qhd->jkhd', score_gradient, query_block) * score_scale
        value_terms = jnp.einsum('hqjk,qhd->jkhd', attention_weight, grad_block)
        key_acc = key_acc.at[chosen].add(key_terms)
        value_acc = value_acc.at[chosen].add(value_terms)
        return ((key_acc, value_acc), (output, grad_qnorm))
    empty = jnp.zeros((block_count, BLOCK, HEADS, head_dim), jnp.float32)
    (key_acc, value_acc), (outputs, grad_qnorms) = lax.scan(block_step, (empty, empty), jnp.arange(block_count, dtype=jnp.int32))
    output = outputs.reshape(tokens, row_width)
    grad_query = norm_back(grad_qnorms.reshape(tokens, HEADS, head_dim), q_normed, q_inverse, gain_query)
    grad_key = norm_back(key_acc.reshape(tokens, HEADS, head_dim), k_normed, k_inverse, gain_key)
    grad_value = value_acc.astype(jnp.bfloat16).reshape(tokens, row_width)
    return (output, grad_query.astype(jnp.bfloat16).reshape(tokens, row_width), grad_key.astype(jnp.bfloat16).reshape(tokens, row_width), grad_value)
```

```python
import functools

import jax
import jax.numpy as jnp
from jax import lax
from jax.experimental import pallas as pl
from jax.experimental.pallas import tpu as pltpu
from jax.sharding import PartitionSpec as P


HEADS = 2
BLOCK = 128
BAND = 2
LEVELS = 4
SLOTS = 7
AXES = ("grp", "ctx")
EPS = 1e-05
F32 = jnp.float32
BF16 = jnp.bfloat16

NT = (((1,), (1,)), ((), ()))
NN = (((1,), (0,)), ((), ()))
TN = (((0,), (0,)), ((), ()))


def dot(a, b, dims):
    return lax.dot_general(a, b, dims, preferred_element_type=F32)


def norm(raw, gain):
    x = raw.astype(F32)
    centred = x - jnp.mean(x, axis=-1, keepdims=True)
    inverse = lax.rsqrt(jnp.mean(centred * centred, axis=-1, keepdims=True) + EPS)
    normed = centred * inverse
    return normed, inverse, normed * gain


def norm_back(upstream, normed, inverse, gain):
    scaled = upstream * gain
    first = jnp.mean(scaled, axis=-1, keepdims=True)
    second = jnp.mean(scaled * normed, axis=-1, keepdims=True)
    return (scaled - first - normed * second) * inverse


def cols(h):
    return slice(h * 128, (h + 1) * 128)


def rows(i):
    return slice(i * BLOCK, (i + 1) * BLOCK)


def picked(ref, kind, pick, h):
    return ref[kind, pl.ds(pl.multiple_of(pick * BLOCK, BLOCK), BLOCK), cols(h)]


def prep_kernel(k_ref, v_ref, gain_ref, pack_ref):
    for h in range(HEADS):
        _, _, scaled = norm(k_ref[:, cols(h)], gain_ref[h : h + 1, :])
        pack_ref[0, :, cols(h)] = scaled.astype(BF16)
    pack_ref[1] = v_ref[...]


def local_kernel(
    dev_ref, reach_ref, part_ref, q_ref, gain_ref, cot_ref, own, left, right, x2, x1,
    qn_ref, e_ref, d_ref, o_ref, l_ref, *, last_block,
):
    scale = 128 ** (-0.5)
    for h in range(HEADS):
        _, _, scaled = norm(q_ref[:, cols(h)], gain_ref[h : h + 1, :])
        qn = scaled.astype(BF16)
        qn_ref[:, cols(h)] = qn
        ct = cot_ref[:, cols(h)]
        near = (left, own, right)
        s_near = [dot(qn, r[0, :, cols(h)], NT) for r in near]
        d_near = [dot(ct, r[1, :, cols(h)], NT) for r in near]
        for i in range(2):
            block = dev_ref[0] * 2 + i
            total = None
            e_list = []
            for slot in range(SLOTS):
                if slot < 5:
                    c = i + slot
                    s = s_near[c // 2][rows(i), rows(c % 2)]
                    d = d_near[c // 2][rows(i), rows(c % 2)]
                else:
                    ref = (x2, x1)[slot - 5]
                    pick = part_ref[i, slot - 5] & 1
                    s = dot(qn[rows(i)], picked(ref, 0, pick, h), NT)
                    d = dot(ct[rows(i)], picked(ref, 1, pick, h), NT)
                e = jnp.exp(s * scale)
                if slot < 5 and slot != 2:
                    off = slot - BAND
                    goal = block + off
                    ok = (abs(off) <= reach_ref[i]) & (goal >= 0) & (goal <= last_block)
                    e = e * jnp.where(ok, 1.0, 0.0).astype(F32)
                total = e if total is None else total + e
                low = e.astype(BF16)
                e_list.append(low)
                e_ref[h, slot, rows(i), :] = low
                d_ref[h, slot, rows(i), :] = d.astype(BF16)
            l_ref[h, rows(i), :] = jnp.broadcast_to(
                jnp.sum(total, axis=-1, keepdims=True), (BLOCK, 128)
            )
            v_list = [near[(i + s) // 2][1, rows((i + s) % 2), cols(h)] for s in range(5)]
            v_list += [picked(r, 1, part_ref[i, n] & 1, h) for n, r in enumerate((x2, x1))]
            o_ref[rows(i), cols(h)] = dot(
                jnp.concatenate(e_list, axis=1), jnp.concatenate(v_list, axis=0), NN
            )


def spread(terms, picks, g):
    parts = [t * jnp.where(p == g, 1.0, 0.0).astype(F32) for t, p in zip(terms, picks)]
    return (parts[0] + parts[1]).astype(BF16)


def far_kernel(
    part_ref, qn_ref, cot_ref, y2, y1, o_ref, l_ref,
    g2_ref, g1_ref, out_ref, rl_ref, delta_ref, dq_ref,
):
    scale = 128 ** (-0.5)
    for h in range(HEADS):
        k_terms = [[], []]
        v_terms = [[], []]
        for i in range(2):
            q = qn_ref[rows(i), cols(h)]
            ct = cot_ref[rows(i), cols(h)]
            picks = [part_ref[i, 2] & 1, part_ref[i, 3] & 1]
            ks = jnp.concatenate([picked(r, 0, p, h) for r, p in zip((y2, y1), picks)], axis=0)
            vs = jnp.concatenate([picked(r, 1, p, h) for r, p in zip((y2, y1), picks)], axis=0)
            e = jnp.exp(dot(q, ks, NT) * scale)
            dp = dot(ct, vs, NT)
            total = l_ref[h, rows(i), :1] + jnp.sum(e, axis=-1, keepdims=True)
            rl = 1.0 / total
            o = ((o_ref[rows(i), cols(h)] + dot(e.astype(BF16), vs, NN)) * rl).astype(BF16)
            out_ref[rows(i), cols(h)] = o
            delta = jnp.sum(ct.astype(F32) * o.astype(F32), axis=-1, keepdims=True)
            rl_ref[h, rows(i), :] = jnp.broadcast_to(rl, (BLOCK, 128))
            delta_ref[h, rows(i), :] = jnp.broadcast_to(delta, (BLOCK, 128))
            p = e * rl
            w = p.astype(BF16)
            ds = (p * (dp - delta)).astype(BF16)
            dq_ref[rows(i), cols(h)] = dot(ds, ks, NN)
            dk = dot(ds, q, TN) * scale
            dv = dot(w, ct, TN)
            for n in range(2):
                k_terms[n].append(dk[rows(n)])
                v_terms[n].append(dv[rows(n)])
        for n, ref in enumerate((g2_ref, g1_ref)):
            picks = [part_ref[i, 2 + n] & 1 for i in range(2)]
            for g in range(2):
                ref[0, rows(g), cols(h)] = spread(k_terms[n], picks, g)
                ref[1, rows(g), cols(h)] = spread(v_terms[n], picks, g)


def near_kernel(
    part_ref, q_ref, gain_ref, qn_ref, cot_ref, own, left, right, x2, x1, e_ref, d_ref,
    rl_ref, delta_ref, dqy_ref,
    gx2_ref, gx1_ref, gl_ref, gr_ref, gown_ref, gq_ref,
):
    scale = 128 ** (-0.5)
    near = (left, own, right)
    for h in range(HEADS):
        qn = qn_ref[:, cols(h)]
        ct = cot_ref[:, cols(h)]
        weights, grads = [], []
        for slot in range(SLOTS):
            p = e_ref[h, slot].astype(F32) * rl_ref[h]
            weights.append(p.astype(BF16))
            grads.append((p * (d_ref[h, slot].astype(F32) - delta_ref[h])).astype(BF16))
        for n, (src, ref) in enumerate(((x2, gx2_ref), (x1, gx1_ref))):
            slot = 5 + n
            picks = [part_ref[i, n] & 1 for i in range(2)]
            k_terms = [dot(grads[slot][rows(i)], qn[rows(i)], TN) * scale for i in range(2)]
            v_terms = [dot(weights[slot][rows(i)], ct[rows(i)], TN) for i in range(2)]
            for g in range(2):
                ref[0, rows(g), cols(h)] = spread(k_terms, picks, g)
                ref[1, rows(g), cols(h)] = spread(v_terms, picks, g)
        for c in range(6):
            picked_rows = [i for i in range(2) if 0 <= c - i < 5]
            span = slice(picked_rows[0] * BLOCK, (picked_rows[-1] + 1) * BLOCK)
            ds = jnp.concatenate([grads[c - i][rows(i)] for i in picked_rows], axis=0)
            w = jnp.concatenate([weights[c - i][rows(i)] for i in picked_rows], axis=0)
            dk = dot(ds, qn[span], TN) * scale
            dv = dot(w, ct[span], TN)
            ref = (gl_ref, gown_ref, gr_ref)[c // 2]
            ref[0, rows(c % 2), cols(h)] = dk.astype(ref.dtype)
            ref[1, rows(c % 2), cols(h)] = dv.astype(ref.dtype)
        normed, inverse, _ = norm(q_ref[:, cols(h)], gain_ref[h : h + 1, :])
        for i in range(2):
            k_list = [near[(i + s) // 2][0, rows((i + s) % 2), cols(h)] for s in range(5)]
            k_list += [picked(r, 0, part_ref[i, n] & 1, h) for n, r in enumerate((x2, x1))]
            dq = dot(
                jnp.concatenate([g[rows(i)] for g in grads], axis=1),
                jnp.concatenate(k_list, axis=0),
                NN,
            )
            dq = (dq + dqy_ref[rows(i), cols(h)]) * scale
            gq_ref[rows(i), cols(h)] = norm_back(
                dq, normed[rows(i)], inverse[rows(i)], gain_ref[h : h + 1, :]
            ).astype(BF16)


def final_kernel(k_ref, gain_ref, own, a, b, c, d, e, f, gk_ref, gv_ref):
    terms = (a, b, c, d, e, f)
    for h in range(HEADS):
        dk = own[0, :, cols(h)]
        dv = own[1, :, cols(h)]
        for t in terms:
            dk = dk + t[0, :, cols(h)].astype(F32)
            dv = dv + t[1, :, cols(h)].astype(F32)
        normed, inverse, _ = norm(k_ref[:, cols(h)], gain_ref[h : h + 1, :])
        gk_ref[:, cols(h)] = norm_back(dk, normed, inverse, gain_ref[h : h + 1, :]).astype(BF16)
        gv_ref[:, cols(h)] = dv.astype(BF16)


V = pl.BlockSpec(memory_space=pltpu.VMEM)
S = pl.BlockSpec(memory_space=pltpu.SMEM)


def call(kernel, specs, outs, flops, *args):
    shapes = [jax.ShapeDtypeStruct(s, t) for s, t in outs]
    moved = sum(a.size * a.dtype.itemsize for a in args)
    moved += sum(s.size * s.dtype.itemsize for s in shapes)
    return pl.pallas_call(
        kernel,
        out_shape=shapes,
        in_specs=specs,
        out_specs=[V] * len(shapes),
        compiler_params=pltpu.CompilerParams(vmem_limit_bytes=24 * 2**20),
        cost_estimate=pl.CostEstimate(flops=flops, transcendentals=0, bytes_accessed=moved),
    )(*args)


def body(query_raw, key_raw, values, band_reach, partners, gain_query, gain_key, cotangent):
    count = lax.axis_size(AXES)
    device = lax.axis_index(AXES).astype(jnp.int32).reshape(1)
    ups = [(i, i + 1) for i in range(count - 1)]
    downs = [(b, a) for a, b in ups]
    masks = [count >> (level + 1) for level in range(LEVELS)]
    across = [[(i, i ^ m) for i in range(count)] for m in masks]

    def send(value, perm):
        return lax.ppermute(value, AXES, perm)

    pack_t = ((2, 256, 256), BF16)

    (pack,) = call(prep_kernel, [V, V, V], [pack_t], 10**6, key_raw, values, gain_key)
    y2 = send(pack, across[2])
    y1 = send(pack, across[3])
    x2 = send(pack, across[0])
    x1 = send(pack, across[1])
    left = send(pack, ups)
    right = send(pack, downs)

    tiles = ((HEADS, SLOTS, 256, 128), BF16)
    rowstat = ((HEADS, 256, 128), F32)
    full = ((256, 256), F32)
    qn, e, d, o_part, l_part = call(
        functools.partial(local_kernel, last_block=2 * count - 1),
        [S, S, S] + [V] * 8,
        [((256, 256), BF16), tiles, tiles, full, rowstat],
        28 * 3 * 2 * 128**3,
        device, band_reach, partners, query_raw, gain_query, cotangent, pack, left, right, x2, x1,
    )
    gy2, gy1, out, rl, delta, dqy = call(
        far_kernel,
        [S] + [V] * 6,
        [pack_t, pack_t, ((256, 256), BF16), rowstat, rowstat, full],
        8 * 6 * 2 * 128**3,
        partners, qn, cotangent, y2, y1, o_part, l_part,
    )
    ry2 = send(gy2, across[2])
    ry1 = send(gy1, across[3])
    gx2, gx1, gl, gr, gown, grad_query = call(
        near_kernel,
        [S] + [V] * 14,
        [pack_t, pack_t, pack_t, pack_t, ((2, 256, 256), F32), ((256, 256), BF16)],
        28 * 3 * 2 * 128**3,
        partners, query_raw, gain_query, qn, cotangent, pack, left, right, x2, x1, e, d,
        rl, delta, dqy,
    )
    rx2 = send(gx2, across[0])
    rx1 = send(gx1, across[1])
    rl_ = send(gr, ups)
    rr_ = send(gl, downs)
    grad_key, grad_value = call(
        final_kernel,
        [V] * 9,
        [((256, 256), BF16), ((256, 256), BF16)],
        10**6,
        key_raw, gain_key, gown, ry2, ry1, rx2, rx1, rl_, rr_,
    )
    return (out, grad_query, grad_key, grad_value)


def solution(mesh):
    wide = P(AXES, None)
    return jax.shard_map(
        body,
        mesh=mesh,
        in_specs=(wide, wide, wide, P(AXES), wide, P(), P(), wide),
        out_specs=(wide, wide, wide, wide),
        check_vma=False,
    )
```

```python
import functools

import jax
import jax.numpy as jnp
from jax import lax
from jax.experimental import pallas as pl
from jax.experimental.pallas import tpu as pltpu
from jax.sharding import PartitionSpec as P


HEADS = 2
BLOCK = 128
BAND = 2
LEVELS = 4
BANDS = 2 * BAND + 1
AXES = ("grp", "ctx")
EPS = 1e-05
F32 = jnp.float32
BF16 = jnp.bfloat16

NT = (((1,), (1,)), ((), ()))
NN = (((1,), (0,)), ((), ()))
TN = (((0,), (0,)), ((), ()))


def dot(a, b, dims):
    return lax.dot_general(a, b, dims, preferred_element_type=F32)


def norm(raw, gain):
    x = raw.astype(F32)
    centred = x - jnp.mean(x, axis=-1, keepdims=True)
    inverse = lax.rsqrt(jnp.mean(centred * centred, axis=-1, keepdims=True) + EPS)
    normed = centred * inverse
    return normed, inverse, normed * gain


def norm_back(upstream, normed, inverse, gain):
    scaled = upstream * gain
    first = jnp.mean(scaled, axis=-1, keepdims=True)
    second = jnp.mean(scaled * normed, axis=-1, keepdims=True)
    return (scaled - first - normed * second) * inverse


def cols(h):
    return slice(h * 128, (h + 1) * 128)


def rows(i):
    return slice(i * BLOCK, (i + 1) * BLOCK)


def picked(ref, kind, pick, h):
    return ref[kind, pl.ds(pl.multiple_of(pick * BLOCK, BLOCK), BLOCK), cols(h)]


def prep_kernel(k_hbm, v_hbm, gain_hbm, pack_ref, k_ref, gain_ref, sems):
    copies = [
        pltpu.make_async_copy(k_hbm, k_ref, sems.at[0]),
        pltpu.make_async_copy(gain_hbm, gain_ref, sems.at[1]),
        pltpu.make_async_copy(v_hbm, pack_ref.at[1], sems.at[2]),
    ]
    for copy in copies:
        copy.start()
    copies[0].wait()
    copies[1].wait()
    for h in range(HEADS):
        _, _, scaled = norm(k_ref[:, cols(h)], gain_ref[h : h + 1, :])
        pack_ref[0, :, cols(h)] = scaled.astype(BF16)
    copies[2].wait()


def local_kernel(
    dev_ref, reach_ref, part_ref, q_ref, gain_ref, cot_ref, own, left, right,
    qn_ref, e_ref, d_ref, o_ref, l_ref, *, last_block,
):
    scale = 128 ** (-0.5)
    near = (left, own, right)
    both = range(HEADS)
    qn = [norm(q_ref[:, cols(h)], gain_ref[h : h + 1, :])[2].astype(BF16) for h in both]
    ct = [cot_ref[:, cols(h)] for h in both]
    for h in both:
        qn_ref[:, cols(h)] = qn[h]
    s_near = [[dot(qn[h], r[0, :, cols(h)], NT) for r in near] for h in both]
    for h in both:
        d_near = [dot(ct[h], r[1, :, cols(h)], NT) for r in near]
        for i in range(2):
            for slot in range(BANDS):
                c = i + slot
                d_ref[h, slot, rows(i), :] = d_near[c // 2][rows(i), rows(c % 2)].astype(BF16)
    for h in both:
        for i in range(2):
            block = dev_ref[0] * 2 + i
            total = None
            e_list = []
            for slot in range(BANDS):
                c = i + slot
                e = jnp.exp(s_near[h][c // 2][rows(i), rows(c % 2)] * scale)
                if slot != BAND:
                    off = slot - BAND
                    goal = block + off
                    ok = (abs(off) <= reach_ref[i]) & (goal >= 0) & (goal <= last_block)
                    e = e * jnp.where(ok, 1.0, 0.0).astype(F32)
                total = e if total is None else total + e
                low = e.astype(BF16)
                e_list.append(low)
                e_ref[h, slot, rows(i), :] = low
            l_ref[h, rows(i), :] = jnp.broadcast_to(
                jnp.sum(total, axis=-1, keepdims=True), (BLOCK, 128)
            )
            v_list = [near[(i + s) // 2][1, rows((i + s) % 2), cols(h)] for s in range(BANDS)]
            o_ref[rows(i), cols(h)] = dot(
                jnp.concatenate(e_list, axis=1), jnp.concatenate(v_list, axis=0), NN
            )


def spread(terms, picks, g):
    parts = [t * jnp.where(p == g, 1.0, 0.0).astype(F32) for t, p in zip(terms, picks)]
    return (parts[0] + parts[1]).astype(BF16)


def far_kernel(
    part_ref, qn_ref, cot_ref, x2, x1, y2, y1, o_ref, l_ref,
    g2_ref, g1_ref, out_ref, rl_ref, delta_ref, dq_ref, e_ref, d_ref,
):
    scale = 128 ** (-0.5)
    levels = (x2, x1, y2, y1)
    each = [(h, i) for h in range(HEADS) for i in range(2)]
    pick = [[part_ref[i, n] & 1 for n in range(LEVELS)] for i in range(2)]
    q = {(h, i): qn_ref[rows(i), cols(h)] for h, i in each}
    ct = {(h, i): cot_ref[rows(i), cols(h)] for h, i in each}
    ks = {
        (h, i): jnp.concatenate([picked(r, 0, p, h) for r, p in zip(levels, pick[i])], axis=0)
        for h, i in each
    }
    vs = {
        (h, i): jnp.concatenate([picked(r, 1, p, h) for r, p in zip(levels, pick[i])], axis=0)
        for h, i in each
    }
    e = {t: jnp.exp(dot(q[t], ks[t], NT) * scale) for t in each}
    dp = {t: dot(ct[t], vs[t], NT) for t in each}
    low = {t: e[t].astype(BF16) for t in each}
    far_o = {t: dot(low[t], vs[t], NN) for t in each}
    p, ds, rl = {}, {}, {}
    for t in each:
        h, i = t
        total = e[t][:, :128] + e[t][:, 128:256] + e[t][:, 256:384] + e[t][:, 384:]
        total = l_ref[h, rows(i), :1] + jnp.sum(total, axis=-1, keepdims=True)
        rl[t] = 1.0 / total
        o = ((o_ref[rows(i), cols(h)] + far_o[t]) * rl[t]).astype(BF16)
        out_ref[rows(i), cols(h)] = o
        delta = jnp.sum(ct[t].astype(F32) * o.astype(F32), axis=-1, keepdims=True)
        rl_ref[h, rows(i), :] = jnp.broadcast_to(rl[t], (BLOCK, 128))
        delta_ref[h, rows(i), :] = jnp.broadcast_to(delta, (BLOCK, 128))
        y = slice(256, 512)
        p[t] = e[t][:, y] * rl[t]
        ds[t] = (p[t] * (dp[t][:, y] - delta)).astype(BF16)
    dk = {t: dot(ds[t], q[t], TN) * scale for t in each}
    dv = {t: dot(p[t].astype(BF16), ct[t], TN) for t in each}
    for h in range(HEADS):
        for n, ref in enumerate((g2_ref, g1_ref)):
            picks = [pick[i][2 + n] for i in range(2)]
            for g in range(2):
                ref[0, rows(g), cols(h)] = spread([dk[h, i][rows(n)] for i in range(2)], picks, g)
                ref[1, rows(g), cols(h)] = spread([dv[h, i][rows(n)] for i in range(2)], picks, g)
    for t in each:
        h, i = t
        dq_ref[rows(i), cols(h)] = dot(ds[t], ks[t][256:], NN)
        for n in range(2):
            e_ref[h, n, rows(i), :] = low[t][:, rows(n)]
            d_ref[h, n, rows(i), :] = dp[t][:, rows(n)].astype(BF16)


def near_kernel(
    part_ref, q_ref, gain_ref, qn_ref, cot_ref, own, left, right, x2, x1, e_ref, d_ref,
    ex_ref, dx_ref, rl_ref, delta_ref, dqy_ref,
    gx2_ref, gx1_ref, gl_ref, gr_ref, gown_ref, gq_ref,
):
    scale = 128 ** (-0.5)
    near = (left, own, right)
    for h in range(HEADS):
        qn = qn_ref[:, cols(h)]
        ct = cot_ref[:, cols(h)]
        weights, grads = [], []
        tiles = [(e_ref[h, s], d_ref[h, s]) for s in range(BANDS)]
        tiles += [(ex_ref[h, s], dx_ref[h, s]) for s in range(2)]
        for e, d in tiles:
            p = e.astype(F32) * rl_ref[h]
            weights.append(p.astype(BF16))
            grads.append((p * (d.astype(F32) - delta_ref[h])).astype(BF16))
        for n, (src, ref) in enumerate(((x2, gx2_ref), (x1, gx1_ref))):
            slot = BANDS + n
            picks = [part_ref[i, n] & 1 for i in range(2)]
            k_terms = [dot(grads[slot][rows(i)], qn[rows(i)], TN) * scale for i in range(2)]
            v_terms = [dot(weights[slot][rows(i)], ct[rows(i)], TN) for i in range(2)]
            for g in range(2):
                ref[0, rows(g), cols(h)] = spread(k_terms, picks, g)
                ref[1, rows(g), cols(h)] = spread(v_terms, picks, g)
        for c in range(6):
            picked_rows = [i for i in range(2) if 0 <= c - i < 5]
            span = slice(picked_rows[0] * BLOCK, (picked_rows[-1] + 1) * BLOCK)
            ds = jnp.concatenate([grads[c - i][rows(i)] for i in picked_rows], axis=0)
            w = jnp.concatenate([weights[c - i][rows(i)] for i in picked_rows], axis=0)
            dk = dot(ds, qn[span], TN) * scale
            dv = dot(w, ct[span], TN)
            ref = (gl_ref, gown_ref, gr_ref)[c // 2]
            ref[0, rows(c % 2), cols(h)] = dk.astype(ref.dtype)
            ref[1, rows(c % 2), cols(h)] = dv.astype(ref.dtype)
        normed, inverse, _ = norm(q_ref[:, cols(h)], gain_ref[h : h + 1, :])
        for i in range(2):
            k_list = [near[(i + s) // 2][0, rows((i + s) % 2), cols(h)] for s in range(5)]
            k_list += [picked(r, 0, part_ref[i, n] & 1, h) for n, r in enumerate((x2, x1))]
            dq = dot(
                jnp.concatenate([g[rows(i)] for g in grads], axis=1),
                jnp.concatenate(k_list, axis=0),
                NN,
            )
            dq = (dq + dqy_ref[rows(i), cols(h)]) * scale
            gq_ref[rows(i), cols(h)] = norm_back(
                dq, normed[rows(i)], inverse[rows(i)], gain_ref[h : h + 1, :]
            ).astype(BF16)


def final_kernel(k_ref, gain_ref, own, a, b, c, d, e, f, gk_ref, gv_ref):
    terms = (a, b, c, d, e, f)
    for h in range(HEADS):
        dk = own[0, :, cols(h)]
        dv = own[1, :, cols(h)]
        for t in terms:
            dk = dk + t[0, :, cols(h)].astype(F32)
            dv = dv + t[1, :, cols(h)].astype(F32)
        normed, inverse, _ = norm(k_ref[:, cols(h)], gain_ref[h : h + 1, :])
        gk_ref[:, cols(h)] = norm_back(dk, normed, inverse, gain_ref[h : h + 1, :]).astype(BF16)
        gv_ref[:, cols(h)] = dv.astype(BF16)


V = pl.BlockSpec(memory_space=pltpu.VMEM)
S = pl.BlockSpec(memory_space=pltpu.SMEM)
H = pl.BlockSpec(memory_space=pltpu.HBM)


def call(kernel, specs, outs, flops, *args, scratch=()):
    shapes = [jax.ShapeDtypeStruct(s, t) for s, t in outs]
    moved = sum(a.size * a.dtype.itemsize for a in args)
    moved += sum(s.size * s.dtype.itemsize for s in shapes)
    return pl.pallas_call(
        kernel,
        out_shape=shapes,
        in_specs=specs,
        out_specs=[V] * len(shapes),
        scratch_shapes=scratch,
        compiler_params=pltpu.CompilerParams(vmem_limit_bytes=24 * 2**20),
        cost_estimate=pl.CostEstimate(flops=flops, transcendentals=0, bytes_accessed=moved),
    )(*args)


def body(query_raw, key_raw, values, band_reach, partners, gain_query, gain_key, cotangent):
    count = lax.axis_size(AXES)
    device = lax.axis_index(AXES).astype(jnp.int32).reshape(1)
    ups = [(i, i + 1) for i in range(count - 1)]
    downs = [(b, a) for a, b in ups]
    masks = [count >> (level + 1) for level in range(LEVELS)]
    across = [[(i, i ^ m) for i in range(count)] for m in masks]

    def send(value, perm):
        return lax.ppermute(value, AXES, perm)

    pack_t = ((2, 256, 256), BF16)

    (pack,) = call(
        prep_kernel, [H, H, H], [pack_t], 10**6,
        *[pltpu.with_memory_space_constraint(a, pltpu.HBM) for a in (key_raw, values, gain_key)],
        scratch=[
            pltpu.VMEM((256, 256), BF16), pltpu.VMEM((HEADS, 128), F32),
            pltpu.SemaphoreType.DMA((3,)),
        ],
    )
    y2 = send(pack, across[2])
    y1 = send(pack, across[3])
    x2 = send(pack, across[0])
    x1 = send(pack, across[1])
    left = send(pack, ups)
    right = send(pack, downs)

    tiles = ((HEADS, BANDS, 256, 128), BF16)
    x_tiles = ((HEADS, 2, 256, 128), BF16)
    rowstat = ((HEADS, 256, 128), F32)
    full = ((256, 256), F32)
    qn, e, d, o_part, l_part = call(
        functools.partial(local_kernel, last_block=2 * count - 1),
        [S, S, S] + [V] * 6,
        [((256, 256), BF16), tiles, tiles, full, rowstat],
        20 * 3 * 2 * 128**3,
        device, band_reach, partners, query_raw, gain_query, cotangent, pack, left, right,
    )
    gy2, gy1, out, rl, delta, dqy, ex, dx = call(
        far_kernel,
        [S] + [V] * 8,
        [pack_t, pack_t, ((256, 256), BF16), rowstat, rowstat, full, x_tiles, x_tiles],
        8 * 9 * 2 * 128**3,
        partners, qn, cotangent, x2, x1, y2, y1, o_part, l_part,
    )
    ry2 = send(gy2, across[2])
    ry1 = send(gy1, across[3])
    gx2, gx1, gl, gr, gown, grad_query = call(
        near_kernel,
        [S] + [V] * 16,
        [pack_t, pack_t, pack_t, pack_t, ((2, 256, 256), F32), ((256, 256), BF16)],
        28 * 3 * 2 * 128**3,
        partners, query_raw, gain_query, qn, cotangent, pack, left, right, x2, x1, e, d,
        ex, dx, rl, delta, dqy,
    )
    rx2 = send(gx2, across[0])
    rx1 = send(gx1, across[1])
    rl_ = send(gr, ups)
    rr_ = send(gl, downs)
    grad_key, grad_value = call(
        final_kernel,
        [V] * 9,
        [((256, 256), BF16), ((256, 256), BF16)],
        10**6,
        key_raw, gain_key, gown, ry2, ry1, rx2, rx1, rl_, rr_,
    )
    return (out, grad_query, grad_key, grad_value)


def solution(mesh):
    wide = P(AXES, None)
    return jax.shard_map(
        body,
        mesh=mesh,
        in_specs=(wide, wide, wide, P(AXES), wide, P(), P(), wide),
        out_specs=(wide, wide, wide, wide),
        check_vma=False,
    )
```

```python
import functools

import jax
import jax.numpy as jnp
from jax import lax
from jax.experimental import pallas as pl
from jax.experimental.pallas import tpu as pltpu
from jax.sharding import PartitionSpec as P


HEADS = 2
BLOCK = 128
LEVELS = 4
AXES = ("grp", "ctx")
EPS = 1e-05
F32 = jnp.float32
BF16 = jnp.bfloat16

NT = (((1,), (1,)), ((), ()))
NN = (((1,), (0,)), ((), ()))
TN = (((0,), (0,)), ((), ()))


def dot(a, b, dims):
    return lax.dot_general(a, b, dims, preferred_element_type=F32)


def norm(raw, gain):
    x = raw.astype(F32)
    centred = x - jnp.mean(x, axis=-1, keepdims=True)
    inverse = lax.rsqrt(jnp.mean(centred * centred, axis=-1, keepdims=True) + EPS)
    normed = centred * inverse
    return normed, inverse, normed * gain


def norm_back(upstream, normed, inverse, gain):
    scaled = upstream * gain
    first = jnp.mean(scaled, axis=-1, keepdims=True)
    second = jnp.mean(scaled * normed, axis=-1, keepdims=True)
    return (scaled - first - normed * second) * inverse


def cols(h):
    return slice(h * 128, (h + 1) * 128)


def rows(i):
    return slice(i * BLOCK, (i + 1) * BLOCK)


def picked(ref, kind, pick, h):
    return ref[kind, pl.ds(pl.multiple_of(pick * BLOCK, BLOCK), BLOCK), cols(h)]


def prep_kernel(k_hbm, v_hbm, gain_hbm, pack_ref, k_ref, gain_ref, sems):
    copies = [
        pltpu.make_async_copy(k_hbm, k_ref, sems.at[0]),
        pltpu.make_async_copy(gain_hbm, gain_ref, sems.at[1]),
        pltpu.make_async_copy(v_hbm, pack_ref.at[1], sems.at[2]),
    ]
    for copy in copies:
        copy.start()
    copies[0].wait()
    copies[1].wait()
    for h in range(HEADS):
        _, _, scaled = norm(k_ref[:, cols(h)], gain_ref[h : h + 1, :])
        pack_ref[0, :, cols(h)] = scaled.astype(BF16)
    copies[2].wait()


def local_kernel(
    dev_ref, reach_ref, part_ref, q_ref, gain_ref, cot_ref, own, mate, beside,
    qn_ref, e_ref, d_ref, o_ref, l_ref, *, last_block,
):
    scale = 128 ** (-0.5)
    near = (own, mate, beside)
    both = range(HEADS)
    step = 1 - 2 * (dev_ref[0] & 1)
    shifts = (0, 2 * step, -2 * step)
    qn = [norm(q_ref[:, cols(h)], gain_ref[h : h + 1, :])[2].astype(BF16) for h in both]
    ct = [cot_ref[:, cols(h)] for h in both]
    for h in both:
        qn_ref[:, cols(h)] = qn[h]
    s_near = [[dot(qn[h], r[0, :, cols(h)], NT) for r in near] for h in both]
    for h in both:
        for n, r in enumerate(near):
            d_ref[h, n] = dot(ct[h], r[1, :, cols(h)], NT).astype(BF16)
    keep = {}
    for i in range(2):
        block = dev_ref[0] * 2 + i
        for n in range(3):
            for g in range(2):
                off = shifts[n] + (g - i)
                goal = block + off
                ok = (jnp.abs(off) <= reach_ref[i]) & (goal >= 0) & (goal <= last_block)
                keep[i, n, g] = jnp.where(ok, 1.0, 0.0).astype(F32)
    for h in both:
        for i in range(2):
            total = None
            for n in range(3):
                for g in range(2):
                    e = jnp.exp(s_near[h][n][rows(i), rows(g)] * scale)
                    if n or g != i:
                        e = e * keep[i, n, g]
                    total = e if total is None else total + e
                    e_ref[h, n, rows(i), rows(g)] = e.astype(BF16)
            l_ref[h, rows(i), :] = jnp.broadcast_to(
                jnp.sum(total, axis=-1, keepdims=True), (BLOCK, 128)
            )
        o_ref[:, cols(h)] = dot(
            jnp.concatenate([e_ref[h, n] for n in range(3)], axis=1),
            jnp.concatenate([r[1, :, cols(h)] for r in near], axis=0),
            NN,
        )


def spread(terms, picks, g):
    parts = [t * jnp.where(p == g, 1.0, 0.0).astype(F32) for t, p in zip(terms, picks)]
    return (parts[0] + parts[1]).astype(BF16)


def far_kernel(
    part_ref, qn_ref, cot_ref, x2, x1, y2, y1, o_ref, l_ref,
    g2_ref, g1_ref, out_ref, rl_ref, delta_ref, dq_ref, e_ref, d_ref,
):
    scale = 128 ** (-0.5)
    levels = (x2, x1, y2, y1)
    each = [(h, i) for h in range(HEADS) for i in range(2)]
    pick = [[part_ref[i, n] & 1 for n in range(LEVELS)] for i in range(2)]
    q = {(h, i): qn_ref[rows(i), cols(h)] for h, i in each}
    ct = {(h, i): cot_ref[rows(i), cols(h)] for h, i in each}
    ks = {
        (h, i): jnp.concatenate([picked(r, 0, p, h) for r, p in zip(levels, pick[i])], axis=0)
        for h, i in each
    }
    vs = {
        (h, i): jnp.concatenate([picked(r, 1, p, h) for r, p in zip(levels, pick[i])], axis=0)
        for h, i in each
    }
    e = {t: jnp.exp(dot(q[t], ks[t], NT) * scale) for t in each}
    dp = {t: dot(ct[t], vs[t], NT) for t in each}
    low = {t: e[t].astype(BF16) for t in each}
    far_o = {t: dot(low[t], vs[t], NN) for t in each}
    p, ds, rl = {}, {}, {}
    for t in each:
        h, i = t
        total = e[t][:, :128] + e[t][:, 128:256] + e[t][:, 256:384] + e[t][:, 384:]
        total = l_ref[h, rows(i), :1] + jnp.sum(total, axis=-1, keepdims=True)
        rl[t] = 1.0 / total
        o = ((o_ref[rows(i), cols(h)] + far_o[t]) * rl[t]).astype(BF16)
        out_ref[rows(i), cols(h)] = o
        delta = jnp.sum(ct[t].astype(F32) * o.astype(F32), axis=-1, keepdims=True)
        rl_ref[h, rows(i), :] = jnp.broadcast_to(rl[t], (BLOCK, 128))
        delta_ref[h, rows(i), :] = jnp.broadcast_to(delta, (BLOCK, 128))
        y = slice(256, 512)
        p[t] = e[t][:, y] * rl[t]
        ds[t] = (p[t] * (dp[t][:, y] - delta)).astype(BF16)
    dk = {t: dot(ds[t], q[t], TN) * scale for t in each}
    dv = {t: dot(p[t].astype(BF16), ct[t], TN) for t in each}
    for h in range(HEADS):
        for n, ref in enumerate((g2_ref, g1_ref)):
            picks = [pick[i][2 + n] for i in range(2)]
            for g in range(2):
                ref[0, rows(g), cols(h)] = spread([dk[h, i][rows(n)] for i in range(2)], picks, g)
                ref[1, rows(g), cols(h)] = spread([dv[h, i][rows(n)] for i in range(2)], picks, g)
    for t in each:
        h, i = t
        dq_ref[rows(i), cols(h)] = dot(ds[t], ks[t][256:], NN)
        for n in range(2):
            e_ref[h, n, rows(i), :] = low[t][:, rows(n)]
            d_ref[h, n, rows(i), :] = dp[t][:, rows(n)].astype(BF16)


def near_kernel(
    part_ref, q_ref, gain_ref, qn_ref, cot_ref, own, mate, beside, x2, x1, e_ref, d_ref,
    ex_ref, dx_ref, rl_ref, delta_ref, dqy_ref,
    gx2_ref, gx1_ref, gm_ref, gb_ref, gown_ref, gq_ref,
):
    scale = 128 ** (-0.5)
    near = (own, mate, beside)
    pick = [[part_ref[i, n] & 1 for n in range(2)] for i in range(2)]
    for h in range(HEADS):
        qn = qn_ref[:, cols(h)]
        ct = cot_ref[:, cols(h)]
        rl = rl_ref[h]
        delta = delta_ref[h]
        x_grads = []
        for n, ref in enumerate((gx2_ref, gx1_ref)):
            p = ex_ref[h, n].astype(F32) * rl
            w = p.astype(BF16)
            ds = (p * (dx_ref[h, n].astype(F32) - delta)).astype(BF16)
            x_grads.append(ds)
            picks = [pick[i][n] for i in range(2)]
            k_terms = [dot(ds[rows(i)], qn[rows(i)], TN) * scale for i in range(2)]
            v_terms = [dot(w[rows(i)], ct[rows(i)], TN) for i in range(2)]
            for g in range(2):
                ref[0, rows(g), cols(h)] = spread(k_terms, picks, g)
                ref[1, rows(g), cols(h)] = spread(v_terms, picks, g)
        rl2 = jnp.concatenate((rl, rl), axis=1)
        delta2 = jnp.concatenate((delta, delta), axis=1)
        grads = []
        for n, ref in enumerate((gown_ref, gm_ref, gb_ref)):
            p = e_ref[h, n].astype(F32) * rl2
            ds = (p * (d_ref[h, n].astype(F32) - delta2)).astype(BF16)
            grads.append(ds)
            ref[0, :, cols(h)] = (dot(ds, qn, TN) * scale).astype(ref.dtype)
            ref[1, :, cols(h)] = dot(p.astype(BF16), ct, TN).astype(ref.dtype)
        normed, inverse, _ = norm(q_ref[:, cols(h)], gain_ref[h : h + 1, :])
        band = dot(
            jnp.concatenate(grads, axis=1),
            jnp.concatenate([r[0, :, cols(h)] for r in near], axis=0),
            NN,
        )
        for i in range(2):
            dq = dot(
                jnp.concatenate([g[rows(i)] for g in x_grads], axis=1),
                jnp.concatenate([picked(r, 0, p, h) for r, p in zip((x2, x1), pick[i])], axis=0),
                NN,
            )
            dq = (dq + band[rows(i)] + dqy_ref[rows(i), cols(h)]) * scale
            gq_ref[rows(i), cols(h)] = norm_back(
                dq, normed[rows(i)], inverse[rows(i)], gain_ref[h : h + 1, :]
            ).astype(BF16)


def final_kernel(k_ref, gain_ref, own, a, b, c, d, e, f, gk_ref, gv_ref):
    terms = (a, b, c, d, e, f)
    for h in range(HEADS):
        dk = own[0, :, cols(h)]
        dv = own[1, :, cols(h)]
        for t in terms:
            dk = dk + t[0, :, cols(h)].astype(F32)
            dv = dv + t[1, :, cols(h)].astype(F32)
        normed, inverse, _ = norm(k_ref[:, cols(h)], gain_ref[h : h + 1, :])
        gk_ref[:, cols(h)] = norm_back(dk, normed, inverse, gain_ref[h : h + 1, :]).astype(BF16)
        gv_ref[:, cols(h)] = dv.astype(BF16)


V = pl.BlockSpec(memory_space=pltpu.VMEM)
S = pl.BlockSpec(memory_space=pltpu.SMEM)
H = pl.BlockSpec(memory_space=pltpu.HBM)


def call(kernel, specs, outs, flops, *args, scratch=()):
    shapes = [jax.ShapeDtypeStruct(s, t) for s, t in outs]
    moved = sum(a.size * a.dtype.itemsize for a in args)
    moved += sum(s.size * s.dtype.itemsize for s in shapes)
    return pl.pallas_call(
        kernel,
        out_shape=shapes,
        in_specs=specs,
        out_specs=[V] * len(shapes),
        scratch_shapes=scratch,
        compiler_params=pltpu.CompilerParams(vmem_limit_bytes=24 * 2**20),
        cost_estimate=pl.CostEstimate(flops=flops, transcendentals=0, bytes_accessed=moved),
    )(*args)


def body(query_raw, key_raw, values, band_reach, partners, gain_query, gain_key, cotangent):
    count = lax.axis_size(AXES)
    device = lax.axis_index(AXES).astype(jnp.int32).reshape(1)
    mates = [(i, i ^ 1) for i in range(count)]
    besides = [(i, j) for a in range(1, count - 1, 2) for i, j in ((a, a + 1), (a + 1, a))]
    masks = [count >> (level + 1) for level in range(LEVELS)]
    across = [[(i, i ^ m) for i in range(count)] for m in masks]

    def send(value, perm):
        return lax.ppermute(value, AXES, perm)

    pack_t = ((2, 256, 256), BF16)

    (pack,) = call(
        prep_kernel, [H, H, H], [pack_t], 10**6,
        *[pltpu.with_memory_space_constraint(a, pltpu.HBM) for a in (key_raw, values, gain_key)],
        scratch=[
            pltpu.VMEM((256, 256), BF16), pltpu.VMEM((HEADS, 128), F32),
            pltpu.SemaphoreType.DMA((3,)),
        ],
    )
    y2 = send(pack, across[2])
    y1 = send(pack, across[3])
    x2 = send(pack, across[0])
    x1 = send(pack, across[1])
    mate = send(pack, mates)
    beside = send(pack, besides)

    tiles = ((HEADS, 3, 256, 256), BF16)
    x_tiles = ((HEADS, 2, 256, 128), BF16)
    rowstat = ((HEADS, 256, 128), F32)
    full = ((256, 256), F32)
    qn, e, d, o_part, l_part = call(
        functools.partial(local_kernel, last_block=2 * count - 1),
        [S, S, S] + [V] * 6,
        [((256, 256), BF16), tiles, tiles, full, rowstat],
        20 * 3 * 2 * 128**3,
        device, band_reach, partners, query_raw, gain_query, cotangent, pack, mate, beside,
    )
    gy2, gy1, out, rl, delta, dqy, ex, dx = call(
        far_kernel,
        [S] + [V] * 8,
        [pack_t, pack_t, ((256, 256), BF16), rowstat, rowstat, full, x_tiles, x_tiles],
        8 * 9 * 2 * 128**3,
        partners, qn, cotangent, x2, x1, y2, y1, o_part, l_part,
    )
    ry2 = send(gy2, across[2])
    ry1 = send(gy1, across[3])
    gx2, gx1, gm, gb, gown, grad_query = call(
        near_kernel,
        [S] + [V] * 16,
        [pack_t, pack_t, pack_t, pack_t, ((2, 256, 256), F32), ((256, 256), BF16)],
        28 * 3 * 2 * 128**3,
        partners, query_raw, gain_query, qn, cotangent, pack, mate, beside, x2, x1, e, d,
        ex, dx, rl, delta, dqy,
    )
    rx2 = send(gx2, across[0])
    rx1 = send(gx1, across[1])
    rm = send(gm, mates)
    rb = send(gb, besides)
    grad_key, grad_value = call(
        final_kernel,
        [V] * 9,
        [((256, 256), BF16), ((256, 256), BF16)],
        10**6,
        key_raw, gain_key, gown, ry2, ry1, rx2, rx1, rm, rb,
    )
    return (out, grad_query, grad_key, grad_value)


def solution(mesh):
    wide = P(AXES, None)
    return jax.shard_map(
        body,
        mesh=mesh,
        in_specs=(wide, wide, wide, P(AXES), wide, P(), P(), wide),
        out_specs=(wide, wide, wide, wide),
        check_vma=False,
    )
```

```python
import functools

import jax
import jax.numpy as jnp
from jax import lax
from jax.experimental import pallas as pl
from jax.experimental.pallas import tpu as pltpu
from jax.sharding import PartitionSpec as P


HEADS = 2
BLOCK = 128
LEVELS = 4
AXES = ("grp", "ctx")
EPS = 1e-05
F32 = jnp.float32
BF16 = jnp.bfloat16

NT = (((1,), (1,)), ((), ()))
NN = (((1,), (0,)), ((), ()))
TN = (((0,), (0,)), ((), ()))


def dot(a, b, dims):
    return lax.dot_general(a, b, dims, preferred_element_type=F32)


def norm(raw, gain):
    x = raw.astype(F32)
    centred = x - jnp.mean(x, axis=-1, keepdims=True)
    inverse = lax.rsqrt(jnp.mean(centred * centred, axis=-1, keepdims=True) + EPS)
    normed = centred * inverse
    return normed, inverse, normed * gain


def norm_back(upstream, normed, inverse, gain):
    scaled = upstream * gain
    first = jnp.mean(scaled, axis=-1, keepdims=True)
    second = jnp.mean(scaled * normed, axis=-1, keepdims=True)
    return (scaled - first - normed * second) * inverse


def cols(h):
    return slice(h * 128, (h + 1) * 128)


def rows(i):
    return slice(i * BLOCK, (i + 1) * BLOCK)


def picked(ref, kind, pick, h):
    return ref[kind, pl.ds(pl.multiple_of(pick * BLOCK, BLOCK), BLOCK), cols(h)]


def prep_kernel(k_hbm, v_hbm, gain_hbm, pack_ref, k_ref, gain_ref, sems):
    copies = [
        pltpu.make_async_copy(k_hbm, k_ref, sems.at[0]),
        pltpu.make_async_copy(gain_hbm, gain_ref, sems.at[1]),
        pltpu.make_async_copy(v_hbm, pack_ref.at[1], sems.at[2]),
    ]
    for copy in copies:
        copy.start()
    copies[0].wait()
    copies[1].wait()
    for h in range(HEADS):
        _, _, scaled = norm(k_ref[:, cols(h)], gain_ref[h : h + 1, :])
        pack_ref[0, :, cols(h)] = scaled.astype(BF16)
    copies[2].wait()


def near_part(own, mate, zpair, zup, zdown, kind, h):
    beside = zpair[kind, :, cols(h)] + zup[kind, :, cols(h)] + zdown[kind, :, cols(h)]
    return [own[kind, :, cols(h)], mate[kind, :, cols(h)], beside]


def local_kernel(
    dev_ref, reach_ref, part_ref, q_ref, gain_ref, cot_ref, own, mate, zpair, zup, zdown,
    qn_ref, e_ref, d_ref, o_ref, l_ref, *, last_block,
):
    scale = 128 ** (-0.5)
    both = range(HEADS)
    ks, vs = ([near_part(own, mate, zpair, zup, zdown, kind, h) for h in both] for kind in (0, 1))
    step = 1 - 2 * (dev_ref[0] & 1)
    shifts = (0, 2 * step, -2 * step)
    qn = [norm(q_ref[:, cols(h)], gain_ref[h : h + 1, :])[2].astype(BF16) for h in both]
    ct = [cot_ref[:, cols(h)] for h in both]
    for h in both:
        qn_ref[:, cols(h)] = qn[h]
    s_near = [[dot(qn[h], k, NT) for k in ks[h]] for h in both]
    for h in both:
        for n, v in enumerate(vs[h]):
            d_ref[h, n] = dot(ct[h], v, NT).astype(BF16)
    keep = {}
    for i in range(2):
        block = dev_ref[0] * 2 + i
        for n in range(3):
            for g in range(2):
                off = shifts[n] + (g - i)
                goal = block + off
                ok = (jnp.abs(off) <= reach_ref[i]) & (goal >= 0) & (goal <= last_block)
                keep[i, n, g] = jnp.where(ok, 1.0, 0.0).astype(F32)
    for h in both:
        for i in range(2):
            total = None
            for n in range(3):
                for g in range(2):
                    e = jnp.exp(s_near[h][n][rows(i), rows(g)] * scale)
                    if n or g != i:
                        e = e * keep[i, n, g]
                    total = e if total is None else total + e
                    e_ref[h, n, rows(i), rows(g)] = e.astype(BF16)
            l_ref[h, rows(i), :] = jnp.broadcast_to(
                jnp.sum(total, axis=-1, keepdims=True), (BLOCK, 128)
            )
        o_ref[:, cols(h)] = dot(
            jnp.concatenate([e_ref[h, n] for n in range(3)], axis=1),
            jnp.concatenate(vs[h], axis=0),
            NN,
        )


def spread(terms, picks, g):
    parts = [t * jnp.where(p == g, 1.0, 0.0).astype(F32) for t, p in zip(terms, picks)]
    return (parts[0] + parts[1]).astype(BF16)


def far_kernel(
    part_ref, qn_ref, cot_ref, x2, x1, y2, y1, o_ref, l_ref,
    g2_ref, g1_ref, out_ref, rl_ref, delta_ref, dq_ref, e_ref, d_ref,
):
    scale = 128 ** (-0.5)
    levels = (x2, x1, y2, y1)
    each = [(h, i) for h in range(HEADS) for i in range(2)]
    pick = [[part_ref[i, n] & 1 for n in range(LEVELS)] for i in range(2)]
    q = {(h, i): qn_ref[rows(i), cols(h)] for h, i in each}
    ct = {(h, i): cot_ref[rows(i), cols(h)] for h, i in each}
    ks = {
        (h, i): jnp.concatenate([picked(r, 0, p, h) for r, p in zip(levels, pick[i])], axis=0)
        for h, i in each
    }
    vs = {
        (h, i): jnp.concatenate([picked(r, 1, p, h) for r, p in zip(levels, pick[i])], axis=0)
        for h, i in each
    }
    e = {t: jnp.exp(dot(q[t], ks[t], NT) * scale) for t in each}
    dp = {t: dot(ct[t], vs[t], NT) for t in each}
    low = {t: e[t].astype(BF16) for t in each}
    far_o = {t: dot(low[t], vs[t], NN) for t in each}
    p, ds, rl = {}, {}, {}
    for t in each:
        h, i = t
        total = e[t][:, :128] + e[t][:, 128:256] + e[t][:, 256:384] + e[t][:, 384:]
        total = l_ref[h, rows(i), :1] + jnp.sum(total, axis=-1, keepdims=True)
        rl[t] = 1.0 / total
        o = ((o_ref[rows(i), cols(h)] + far_o[t]) * rl[t]).astype(BF16)
        out_ref[rows(i), cols(h)] = o
        delta = jnp.sum(ct[t].astype(F32) * o.astype(F32), axis=-1, keepdims=True)
        rl_ref[h, rows(i), :] = jnp.broadcast_to(rl[t], (BLOCK, 128))
        delta_ref[h, rows(i), :] = jnp.broadcast_to(delta, (BLOCK, 128))
        y = slice(256, 512)
        p[t] = e[t][:, y] * rl[t]
        ds[t] = (p[t] * (dp[t][:, y] - delta)).astype(BF16)
    dk = {t: dot(ds[t], q[t], TN) * scale for t in each}
    dv = {t: dot(p[t].astype(BF16), ct[t], TN) for t in each}
    for h in range(HEADS):
        for n, ref in enumerate((g2_ref, g1_ref)):
            picks = [pick[i][2 + n] for i in range(2)]
            for g in range(2):
                ref[0, rows(g), cols(h)] = spread([dk[h, i][rows(n)] for i in range(2)], picks, g)
                ref[1, rows(g), cols(h)] = spread([dv[h, i][rows(n)] for i in range(2)], picks, g)
    for t in each:
        h, i = t
        dq_ref[rows(i), cols(h)] = dot(ds[t], ks[t][256:], NN)
        for n in range(2):
            e_ref[h, n, rows(i), :] = low[t][:, rows(n)]
            d_ref[h, n, rows(i), :] = dp[t][:, rows(n)].astype(BF16)


def near_kernel(
    part_ref, q_ref, gain_ref, qn_ref, cot_ref, own, mate, zpair, zup, zdown, x2, x1, e_ref, d_ref,
    ex_ref, dx_ref, rl_ref, delta_ref, dqy_ref,
    gx2_ref, gx1_ref, gm_ref, gb_ref, gown_ref, gq_ref,
):
    scale = 128 ** (-0.5)
    pick = [[part_ref[i, n] & 1 for n in range(2)] for i in range(2)]
    for h in range(HEADS):
        qn = qn_ref[:, cols(h)]
        ct = cot_ref[:, cols(h)]
        rl = rl_ref[h]
        delta = delta_ref[h]
        x_grads = []
        for n, ref in enumerate((gx2_ref, gx1_ref)):
            p = ex_ref[h, n].astype(F32) * rl
            w = p.astype(BF16)
            ds = (p * (dx_ref[h, n].astype(F32) - delta)).astype(BF16)
            x_grads.append(ds)
            picks = [pick[i][n] for i in range(2)]
            k_terms = [dot(ds[rows(i)], qn[rows(i)], TN) * scale for i in range(2)]
            v_terms = [dot(w[rows(i)], ct[rows(i)], TN) for i in range(2)]
            for g in range(2):
                ref[0, rows(g), cols(h)] = spread(k_terms, picks, g)
                ref[1, rows(g), cols(h)] = spread(v_terms, picks, g)
        rl2 = jnp.concatenate((rl, rl), axis=1)
        delta2 = jnp.concatenate((delta, delta), axis=1)
        grads = []
        for n, ref in enumerate((gown_ref, gm_ref, gb_ref)):
            p = e_ref[h, n].astype(F32) * rl2
            ds = (p * (d_ref[h, n].astype(F32) - delta2)).astype(BF16)
            grads.append(ds)
            ref[0, :, cols(h)] = (dot(ds, qn, TN) * scale).astype(ref.dtype)
            ref[1, :, cols(h)] = dot(p.astype(BF16), ct, TN).astype(ref.dtype)
        normed, inverse, _ = norm(q_ref[:, cols(h)], gain_ref[h : h + 1, :])
        band = dot(
            jnp.concatenate(grads, axis=1),
            jnp.concatenate(near_part(own, mate, zpair, zup, zdown, 0, h), axis=0),
            NN,
        )
        for i in range(2):
            dq = dot(
                jnp.concatenate([g[rows(i)] for g in x_grads], axis=1),
                jnp.concatenate([picked(r, 0, p, h) for r, p in zip((x2, x1), pick[i])], axis=0),
                NN,
            )
            dq = (dq + band[rows(i)] + dqy_ref[rows(i), cols(h)]) * scale
            gq_ref[rows(i), cols(h)] = norm_back(
                dq, normed[rows(i)], inverse[rows(i)], gain_ref[h : h + 1, :]
            ).astype(BF16)


def final_kernel(k_ref, gain_ref, own, a, b, c, d, e, f, g, h, gk_ref, gv_ref):
    terms = (a, b, c, d, e, f, g, h)
    for n in range(HEADS):
        dk = own[0, :, cols(n)]
        dv = own[1, :, cols(n)]
        for t in terms:
            dk = dk + t[0, :, cols(n)].astype(F32)
            dv = dv + t[1, :, cols(n)].astype(F32)
        normed, inverse, _ = norm(k_ref[:, cols(n)], gain_ref[n : n + 1, :])
        gk_ref[:, cols(n)] = norm_back(dk, normed, inverse, gain_ref[n : n + 1, :]).astype(BF16)
        gv_ref[:, cols(n)] = dv.astype(BF16)


V = pl.BlockSpec(memory_space=pltpu.VMEM)
S = pl.BlockSpec(memory_space=pltpu.SMEM)
H = pl.BlockSpec(memory_space=pltpu.HBM)


def call(kernel, specs, outs, flops, *args, scratch=()):
    shapes = [jax.ShapeDtypeStruct(s, t) for s, t in outs]
    moved = sum(a.size * a.dtype.itemsize for a in args)
    moved += sum(s.size * s.dtype.itemsize for s in shapes)
    return pl.pallas_call(
        kernel,
        out_shape=shapes,
        in_specs=specs,
        out_specs=[V] * len(shapes),
        scratch_shapes=scratch,
        compiler_params=pltpu.CompilerParams(vmem_limit_bytes=24 * 2**20),
        cost_estimate=pl.CostEstimate(flops=flops, transcendentals=0, bytes_accessed=moved),
    )(*args)


def body(query_raw, key_raw, values, band_reach, partners, gain_query, gain_key, cotangent):
    count = lax.axis_size(AXES)
    device = lax.axis_index(AXES).astype(jnp.int32).reshape(1)
    mates = [(i, i ^ 1) for i in range(count)]
    run = lax.axis_size("ctx") // 2
    joints = [(a, a + 1) for a in range(1, count - 1, 2)]
    cross_up = [(a, b) for a, b in joints if a // run != b // run]
    cross_down = [(b, a) for a, b in cross_up]
    inner = [(a, b) for a, b in joints if a // run == b // run]
    inner = [p for a, b in inner for p in ((a, b), (b, a))]
    masks = [count >> (level + 1) for level in range(LEVELS)]
    across = [[(i, i ^ m) for i in range(count)] for m in masks]

    def send(value, perm):
        return lax.ppermute(value, AXES, perm)

    pack_t = ((2, 256, 256), BF16)

    (pack,) = call(
        prep_kernel, [H, H, H], [pack_t], 10**6,
        *[pltpu.with_memory_space_constraint(a, pltpu.HBM) for a in (key_raw, values, gain_key)],
        scratch=[
            pltpu.VMEM((256, 256), BF16), pltpu.VMEM((HEADS, 128), F32),
            pltpu.SemaphoreType.DMA((3,)),
        ],
    )
    y2 = send(pack, across[2])
    y1 = send(pack, across[3])
    x2 = send(pack, across[0])
    x1 = send(pack, across[1])
    mate = send(pack, mates)
    zpair = send(pack, inner)
    zup = send(pack, cross_up)
    zdown = send(pack, cross_down)

    tiles = ((HEADS, 3, 256, 256), BF16)
    x_tiles = ((HEADS, 2, 256, 128), BF16)
    rowstat = ((HEADS, 256, 128), F32)
    full = ((256, 256), F32)
    qn, e, d, o_part, l_part = call(
        functools.partial(local_kernel, last_block=2 * count - 1),
        [S, S, S] + [V] * 8,
        [((256, 256), BF16), tiles, tiles, full, rowstat],
        20 * 3 * 2 * 128**3,
        device, band_reach, partners, query_raw, gain_query, cotangent, pack, mate, zpair, zup, zdown,
    )
    gy2, gy1, out, rl, delta, dqy, ex, dx = call(
        far_kernel,
        [S] + [V] * 8,
        [pack_t, pack_t, ((256, 256), BF16), rowstat, rowstat, full, x_tiles, x_tiles],
        8 * 9 * 2 * 128**3,
        partners, qn, cotangent, x2, x1, y2, y1, o_part, l_part,
    )
    ry2 = send(gy2, across[2])
    ry1 = send(gy1, across[3])
    gx2, gx1, gm, gb, gown, grad_query = call(
        near_kernel,
        [S] + [V] * 18,
        [pack_t, pack_t, pack_t, pack_t, ((2, 256, 256), F32), ((256, 256), BF16)],
        28 * 3 * 2 * 128**3,
        partners, query_raw, gain_query, qn, cotangent, pack, mate, zpair, zup, zdown, x2, x1, e, d,
        ex, dx, rl, delta, dqy,
    )
    rx2 = send(gx2, across[0])
    rx1 = send(gx1, across[1])
    rm = send(gm, mates)
    rb = send(gb, inner)
    ru = send(gb, cross_up)
    rd = send(gb, cross_down)
    grad_key, grad_value = call(
        final_kernel,
        [V] * 11,
        [((256, 256), BF16), ((256, 256), BF16)],
        10**6,
        key_raw, gain_key, gown, ry2, ry1, rx2, rx1, rm, rb, ru, rd,
    )
    return (out, grad_query, grad_key, grad_value)


def solution(mesh):
    wide = P(AXES, None)
    return jax.shard_map(
        body,
        mesh=mesh,
        in_specs=(wide, wide, wide, P(AXES), wide, P(), P(), wide),
        out_specs=(wide, wide, wide, wide),
        check_vma=False,
    )
```

```python
import functools

import jax
import jax.numpy as jnp
from jax import lax
from jax.experimental import pallas as pl
from jax.experimental.pallas import tpu as pltpu
from jax.sharding import PartitionSpec as P


HEADS = 2
BLOCK = 128
LEVELS = 4
AXES = ("grp", "ctx")
EPS = 1e-05
F32 = jnp.float32
BF16 = jnp.bfloat16

NT = (((1,), (1,)), ((), ()))
NN = (((1,), (0,)), ((), ()))
TN = (((0,), (0,)), ((), ()))


def dot(a, b, dims):
    return lax.dot_general(a, b, dims, preferred_element_type=F32)


def norm(raw, gain):
    x = raw.astype(F32)
    centred = x - jnp.mean(x, axis=-1, keepdims=True)
    inverse = lax.rsqrt(jnp.mean(centred * centred, axis=-1, keepdims=True) + EPS)
    normed = centred * inverse
    return normed, inverse, normed * gain


def norm_back(upstream, normed, inverse, gain):
    scaled = upstream * gain
    first = jnp.mean(scaled, axis=-1, keepdims=True)
    second = jnp.mean(scaled * normed, axis=-1, keepdims=True)
    return (scaled - first - normed * second) * inverse


def cols(h):
    return slice(h * 128, (h + 1) * 128)


def rows(i):
    return slice(i * BLOCK, (i + 1) * BLOCK)


def picked(ref, kind, pick, h):
    return ref[kind, pl.ds(pl.multiple_of(pick * BLOCK, BLOCK), BLOCK), cols(h)]


def prep_kernel(k_hbm, v_hbm, gain_hbm, pack_ref, k_ref, gain_ref, sems):
    copies = [
        pltpu.make_async_copy(k_hbm, k_ref, sems.at[0]),
        pltpu.make_async_copy(gain_hbm, gain_ref, sems.at[1]),
        pltpu.make_async_copy(v_hbm, pack_ref.at[1], sems.at[2]),
    ]
    for copy in copies:
        copy.start()
    copies[0].wait()
    copies[1].wait()
    for h in range(HEADS):
        _, _, scaled = norm(k_ref[:, cols(h)], gain_ref[h : h + 1, :])
        pack_ref[0, :, cols(h)] = scaled.astype(BF16)
    copies[2].wait()


def near_part(own, mate, zpair, zup, zdown, kind, h):
    beside = zpair[kind, :, cols(h)] + zup[kind, :, cols(h)] + zdown[kind, :, cols(h)]
    return [own[kind, :, cols(h)], mate[kind, :, cols(h)], beside]


def local_kernel(
    dev_ref, reach_ref, part_ref, q_ref, gain_ref, cot_ref, own, mate, zpair, zup, zdown,
    qn_ref, e_ref, d_ref, o_ref, l_ref, *, last_block,
):
    scale = 128 ** (-0.5)
    both = range(HEADS)
    ks, vs = ([near_part(own, mate, zpair, zup, zdown, kind, h) for h in both] for kind in (0, 1))
    step = 1 - 2 * (dev_ref[0] & 1)
    shifts = (0, 2 * step, -2 * step)
    qn = [norm(q_ref[:, cols(h)], gain_ref[h : h + 1, :])[2].astype(BF16) for h in both]
    ct = [cot_ref[:, cols(h)] for h in both]
    for h in both:
        qn_ref[:, cols(h)] = qn[h]
    s_near = [[dot(qn[h], k, NT) for k in ks[h]] for h in both]
    for h in both:
        for n, v in enumerate(vs[h]):
            d_ref[h, n] = dot(ct[h], v, NT).astype(BF16)
    keep = {}
    for i in range(2):
        block = dev_ref[0] * 2 + i
        for n in range(3):
            for g in range(2):
                off = shifts[n] + (g - i)
                goal = block + off
                ok = (jnp.abs(off) <= reach_ref[i]) & (goal >= 0) & (goal <= last_block)
                keep[i, n, g] = jnp.where(ok, 1.0, 0.0).astype(F32)
    for h in both:
        for i in range(2):
            total = None
            for n in range(3):
                for g in range(2):
                    e = jnp.exp(s_near[h][n][rows(i), rows(g)] * scale)
                    if n or g != i:
                        e = e * keep[i, n, g]
                    total = e if total is None else total + e
                    e_ref[h, n, rows(i), rows(g)] = e.astype(BF16)
            l_ref[h, rows(i), :] = jnp.broadcast_to(
                jnp.sum(total, axis=-1, keepdims=True), (BLOCK, 128)
            )
        o_ref[:, cols(h)] = dot(
            jnp.concatenate([e_ref[h, n] for n in range(3)], axis=1),
            jnp.concatenate(vs[h], axis=0),
            NN,
        )


def spread(terms, picks, g):
    parts = [t * jnp.where(p == g, 1.0, 0.0).astype(F32) for t, p in zip(terms, picks)]
    return (parts[0] + parts[1]).astype(BF16)


def far_kernel(
    part_ref, qn_ref, cot_ref, x2, x1, y2, y1, o_ref, l_ref, eb_ref, db_ref,
    g2_ref, g1_ref, gb_ref, out_ref, rl_ref, delta_ref, dq_ref, e_ref, d_ref,
):
    scale = 128 ** (-0.5)
    levels = (x2, x1, y2, y1)
    each = [(h, i) for h in range(HEADS) for i in range(2)]
    pick = [[part_ref[i, n] & 1 for n in range(LEVELS)] for i in range(2)]
    q = {(h, i): qn_ref[rows(i), cols(h)] for h, i in each}
    ct = {(h, i): cot_ref[rows(i), cols(h)] for h, i in each}
    ks = {
        (h, i): jnp.concatenate([picked(r, 0, p, h) for r, p in zip(levels, pick[i])], axis=0)
        for h, i in each
    }
    vs = {
        (h, i): jnp.concatenate([picked(r, 1, p, h) for r, p in zip(levels, pick[i])], axis=0)
        for h, i in each
    }
    e = {t: jnp.exp(dot(q[t], ks[t], NT) * scale) for t in each}
    dp = {t: dot(ct[t], vs[t], NT) for t in each}
    low = {t: e[t].astype(BF16) for t in each}
    far_o = {t: dot(low[t], vs[t], NN) for t in each}
    p, ds, rl, delta = {}, {}, {}, {}
    for t in each:
        h, i = t
        total = e[t][:, :128] + e[t][:, 128:256] + e[t][:, 256:384] + e[t][:, 384:]
        total = l_ref[h, rows(i), :1] + jnp.sum(total, axis=-1, keepdims=True)
        rl[t] = 1.0 / total
        o = ((o_ref[rows(i), cols(h)] + far_o[t]) * rl[t]).astype(BF16)
        out_ref[rows(i), cols(h)] = o
        delta[t] = jnp.sum(ct[t].astype(F32) * o.astype(F32), axis=-1, keepdims=True)
        rl_ref[h, rows(i), :] = jnp.broadcast_to(rl[t], (BLOCK, 128))
        delta_ref[h, rows(i), :] = jnp.broadcast_to(delta[t], (BLOCK, 128))
        y = slice(256, 512)
        p[t] = e[t][:, y] * rl[t]
        ds[t] = (p[t] * (dp[t][:, y] - delta[t])).astype(BF16)
    dk = {t: dot(ds[t], q[t], TN) * scale for t in each}
    dv = {t: dot(p[t].astype(BF16), ct[t], TN) for t in each}
    for h in range(HEADS):
        for n, ref in enumerate((g2_ref, g1_ref)):
            picks = [pick[i][2 + n] for i in range(2)]
            for g in range(2):
                ref[0, rows(g), cols(h)] = spread([dk[h, i][rows(n)] for i in range(2)], picks, g)
                ref[1, rows(g), cols(h)] = spread([dv[h, i][rows(n)] for i in range(2)], picks, g)
    for h in range(HEADS):
        full = [jnp.concatenate((v[h, 0], v[h, 1]), axis=0) for v in (rl, delta, q, ct)]
        pb = eb_ref[h, 2].astype(F32) * full[0]
        dsb = (pb * (db_ref[h, 2].astype(F32) - full[1])).astype(BF16)
        gb_ref[0, :, cols(h)] = (dot(dsb, full[2], TN) * scale).astype(BF16)
        gb_ref[1, :, cols(h)] = dot(pb.astype(BF16), full[3], TN).astype(BF16)
    for t in each:
        h, i = t
        dq_ref[rows(i), cols(h)] = dot(ds[t], ks[t][256:], NN)
        for n in range(2):
            e_ref[h, n, rows(i), :] = low[t][:, rows(n)]
            d_ref[h, n, rows(i), :] = dp[t][:, rows(n)].astype(BF16)


def near_kernel(
    part_ref, q_ref, gain_ref, qn_ref, cot_ref, own, mate, zpair, zup, zdown, x2, x1, e_ref, d_ref,
    ex_ref, dx_ref, rl_ref, delta_ref, dqy_ref,
    gx2_ref, gx1_ref, gm_ref, gown_ref, gq_ref,
):
    scale = 128 ** (-0.5)
    pick = [[part_ref[i, n] & 1 for n in range(2)] for i in range(2)]
    for h in range(HEADS):
        qn = qn_ref[:, cols(h)]
        ct = cot_ref[:, cols(h)]
        rl = rl_ref[h]
        delta = delta_ref[h]
        x_grads = []
        for n, ref in enumerate((gx2_ref, gx1_ref)):
            p = ex_ref[h, n].astype(F32) * rl
            w = p.astype(BF16)
            ds = (p * (dx_ref[h, n].astype(F32) - delta)).astype(BF16)
            x_grads.append(ds)
            picks = [pick[i][n] for i in range(2)]
            k_terms = [dot(ds[rows(i)], qn[rows(i)], TN) * scale for i in range(2)]
            v_terms = [dot(w[rows(i)], ct[rows(i)], TN) for i in range(2)]
            for g in range(2):
                ref[0, rows(g), cols(h)] = spread(k_terms, picks, g)
                ref[1, rows(g), cols(h)] = spread(v_terms, picks, g)
        rl2 = jnp.concatenate((rl, rl), axis=1)
        delta2 = jnp.concatenate((delta, delta), axis=1)
        grads = []
        for n, ref in enumerate((gown_ref, gm_ref, None)):
            p = e_ref[h, n].astype(F32) * rl2
            ds = (p * (d_ref[h, n].astype(F32) - delta2)).astype(BF16)
            grads.append(ds)
            if ref is None:
                continue
            ref[0, :, cols(h)] = (dot(ds, qn, TN) * scale).astype(ref.dtype)
            ref[1, :, cols(h)] = dot(p.astype(BF16), ct, TN).astype(ref.dtype)
        normed, inverse, _ = norm(q_ref[:, cols(h)], gain_ref[h : h + 1, :])
        band = dot(
            jnp.concatenate(grads, axis=1),
            jnp.concatenate(near_part(own, mate, zpair, zup, zdown, 0, h), axis=0),
            NN,
        )
        for i in range(2):
            dq = dot(
                jnp.concatenate([g[rows(i)] for g in x_grads], axis=1),
                jnp.concatenate([picked(r, 0, p, h) for r, p in zip((x2, x1), pick[i])], axis=0),
                NN,
            )
            dq = (dq + band[rows(i)] + dqy_ref[rows(i), cols(h)]) * scale
            gq_ref[rows(i), cols(h)] = norm_back(
                dq, normed[rows(i)], inverse[rows(i)], gain_ref[h : h + 1, :]
            ).astype(BF16)


def final_kernel(k_ref, gain_ref, own, a, b, c, d, e, f, g, h, gk_ref, gv_ref):
    terms = (a, b, c, d, e, f, g, h)
    for n in range(HEADS):
        dk = own[0, :, cols(n)]
        dv = own[1, :, cols(n)]
        for t in terms:
            dk = dk + t[0, :, cols(n)].astype(F32)
            dv = dv + t[1, :, cols(n)].astype(F32)
        normed, inverse, _ = norm(k_ref[:, cols(n)], gain_ref[n : n + 1, :])
        gk_ref[:, cols(n)] = norm_back(dk, normed, inverse, gain_ref[n : n + 1, :]).astype(BF16)
        gv_ref[:, cols(n)] = dv.astype(BF16)


V = pl.BlockSpec(memory_space=pltpu.VMEM)
S = pl.BlockSpec(memory_space=pltpu.SMEM)
H = pl.BlockSpec(memory_space=pltpu.HBM)


def call(kernel, specs, outs, flops, *args, scratch=()):
    shapes = [jax.ShapeDtypeStruct(s, t) for s, t in outs]
    moved = sum(a.size * a.dtype.itemsize for a in args)
    moved += sum(s.size * s.dtype.itemsize for s in shapes)
    return pl.pallas_call(
        kernel,
        out_shape=shapes,
        in_specs=specs,
        out_specs=[V] * len(shapes),
        scratch_shapes=scratch,
        compiler_params=pltpu.CompilerParams(vmem_limit_bytes=24 * 2**20),
        cost_estimate=pl.CostEstimate(flops=flops, transcendentals=0, bytes_accessed=moved),
    )(*args)


def body(query_raw, key_raw, values, band_reach, partners, gain_query, gain_key, cotangent):
    count = lax.axis_size(AXES)
    device = lax.axis_index(AXES).astype(jnp.int32).reshape(1)
    mates = [(i, i ^ 1) for i in range(count)]
    run = lax.axis_size("ctx") // 2
    joints = [(a, a + 1) for a in range(1, count - 1, 2)]
    cross_up = [(a, b) for a, b in joints if a // run != b // run]
    cross_down = [(b, a) for a, b in cross_up]
    inner = [(a, b) for a, b in joints if a // run == b // run]
    inner = [p for a, b in inner for p in ((a, b), (b, a))]
    masks = [count >> (level + 1) for level in range(LEVELS)]
    across = [[(i, i ^ m) for i in range(count)] for m in masks]

    def send(value, perm):
        return lax.ppermute(value, AXES, perm)

    pack_t = ((2, 256, 256), BF16)

    (pack,) = call(
        prep_kernel, [H, H, H], [pack_t], 10**6,
        *[pltpu.with_memory_space_constraint(a, pltpu.HBM) for a in (key_raw, values, gain_key)],
        scratch=[
            pltpu.VMEM((256, 256), BF16), pltpu.VMEM((HEADS, 128), F32),
            pltpu.SemaphoreType.DMA((3,)),
        ],
    )
    y2 = send(pack, across[2])
    y1 = send(pack, across[3])
    x2 = send(pack, across[0])
    x1 = send(pack, across[1])
    mate = send(pack, mates)
    zpair = send(pack, inner)
    zup = send(pack, cross_up)
    zdown = send(pack, cross_down)

    tiles = ((HEADS, 3, 256, 256), BF16)
    x_tiles = ((HEADS, 2, 256, 128), BF16)
    rowstat = ((HEADS, 256, 128), F32)
    full = ((256, 256), F32)
    qn, e, d, o_part, l_part = call(
        functools.partial(local_kernel, last_block=2 * count - 1),
        [S, S, S] + [V] * 8,
        [((256, 256), BF16), tiles, tiles, full, rowstat],
        20 * 3 * 2 * 128**3,
        device, band_reach, partners, query_raw, gain_query, cotangent, pack, mate, zpair, zup, zdown,
    )
    gy2, gy1, gb, out, rl, delta, dqy, ex, dx = call(
        far_kernel,
        [S] + [V] * 10,
        [pack_t, pack_t, pack_t, ((256, 256), BF16), rowstat, rowstat, full, x_tiles, x_tiles],
        8 * 9 * 2 * 128**3,
        partners, qn, cotangent, x2, x1, y2, y1, o_part, l_part, e, d,
    )
    ry2 = send(gy2, across[2])
    ry1 = send(gy1, across[3])
    gx2, gx1, gm, gown, grad_query = call(
        near_kernel,
        [S] + [V] * 18,
        [pack_t, pack_t, pack_t, ((2, 256, 256), F32), ((256, 256), BF16)],
        28 * 3 * 2 * 128**3,
        partners, query_raw, gain_query, qn, cotangent, pack, mate, zpair, zup, zdown, x2, x1, e, d,
        ex, dx, rl, delta, dqy,
    )
    rx2 = send(gx2, across[0])
    rx1 = send(gx1, across[1])
    rm = send(gm, mates)
    rb = send(gb, inner)
    ru = send(gb, cross_up)
    rd = send(gb, cross_down)
    grad_key, grad_value = call(
        final_kernel,
        [V] * 11,
        [((256, 256), BF16), ((256, 256), BF16)],
        10**6,
        key_raw, gain_key, gown, ry2, ry1, rx2, rx1, rm, rb, ru, rd,
    )
    return (out, grad_query, grad_key, grad_value)


def solution(mesh):
    wide = P(AXES, None)
    return jax.shard_map(
        body,
        mesh=mesh,
        in_specs=(wide, wide, wide, P(AXES), wide, P(), P(), wide),
        out_specs=(wide, wide, wide, wide),
        check_vma=False,
    )
```

```python
import functools

import jax
import jax.numpy as jnp
from jax import lax
from jax.experimental import pallas as pl
from jax.experimental.pallas import tpu as pltpu
from jax.sharding import PartitionSpec as P


HEADS = 2
BLOCK = 128
LEVELS = 4
AXES = ("grp", "ctx")
EPS = 1e-05
F32 = jnp.float32
BF16 = jnp.bfloat16

NT = (((1,), (1,)), ((), ()))
NN = (((1,), (0,)), ((), ()))
TN = (((0,), (0,)), ((), ()))


def dot(a, b, dims):
    return lax.dot_general(a, b, dims, preferred_element_type=F32)


def norm(raw, gain):
    x = raw.astype(F32)
    centred = x - jnp.mean(x, axis=-1, keepdims=True)
    inverse = lax.rsqrt(jnp.mean(centred * centred, axis=-1, keepdims=True) + EPS)
    normed = centred * inverse
    return normed, inverse, normed * gain


def norm_back(upstream, normed, inverse, gain):
    scaled = upstream * gain
    first = jnp.mean(scaled, axis=-1, keepdims=True)
    second = jnp.mean(scaled * normed, axis=-1, keepdims=True)
    return (scaled - first - normed * second) * inverse


def cols(h):
    return slice(h * 128, (h + 1) * 128)


def rows(i):
    return slice(i * BLOCK, (i + 1) * BLOCK)


def picked(ref, kind, pick, h):
    return ref[kind, pl.ds(pl.multiple_of(pick * BLOCK, BLOCK), BLOCK), cols(h)]


def prep_kernel(k_hbm, v_hbm, gain_hbm, pack_ref, k_ref, gain_ref, sems):
    copies = [
        pltpu.make_async_copy(k_hbm, k_ref, sems.at[0]),
        pltpu.make_async_copy(gain_hbm, gain_ref, sems.at[1]),
        pltpu.make_async_copy(v_hbm, pack_ref.at[1], sems.at[2]),
    ]
    for copy in copies:
        copy.start()
    copies[0].wait()
    copies[1].wait()
    for h in range(HEADS):
        _, _, scaled = norm(k_ref[:, cols(h)], gain_ref[h : h + 1, :])
        pack_ref[0, :, cols(h)] = scaled.astype(BF16)
    copies[2].wait()


def near_part(own, mate, zpair, zup, zdown, kind, h):
    beside = zpair[kind, :, cols(h)] + zup[kind, :, cols(h)] + zdown[kind, :, cols(h)]
    return [own[kind, :, cols(h)], mate[kind, :, cols(h)], beside]


def local_kernel(
    dev_ref, reach_ref, part_ref, q_ref, gain_ref, cot_ref, own, mate, zpair, zup, zdown,
    qn_ref, e_ref, d_ref, o_ref, l_ref, *, last_block,
):
    scale = 128 ** (-0.5)
    both = range(HEADS)
    ks, vs = ([near_part(own, mate, zpair, zup, zdown, kind, h) for h in both] for kind in (0, 1))
    step = 1 - 2 * (dev_ref[0] & 1)
    shifts = (0, 2 * step, -2 * step)
    qn = [norm(q_ref[:, cols(h)], gain_ref[h : h + 1, :])[2].astype(BF16) for h in both]
    ct = [cot_ref[:, cols(h)] for h in both]
    for h in both:
        qn_ref[:, cols(h)] = qn[h]
    s_near = [[dot(qn[h], k, NT) for k in ks[h]] for h in both]
    for h in both:
        for n, v in enumerate(vs[h]):
            d_ref[h, n] = dot(ct[h], v, NT).astype(BF16)
    keep = {}
    for i in range(2):
        block = dev_ref[0] * 2 + i
        for n in range(3):
            for g in range(2):
                off = shifts[n] + (g - i)
                goal = block + off
                ok = (jnp.abs(off) <= reach_ref[i]) & (goal >= 0) & (goal <= last_block)
                keep[i, n, g] = jnp.where(ok, 1.0, 0.0).astype(F32)
    for h in both:
        for i in range(2):
            total = None
            for n in range(3):
                for g in range(2):
                    e = jnp.exp(s_near[h][n][rows(i), rows(g)] * scale)
                    if n or g != i:
                        e = e * keep[i, n, g]
                    total = e if total is None else total + e
                    e_ref[h, n, rows(i), rows(g)] = e.astype(BF16)
            l_ref[h, rows(i), :] = jnp.broadcast_to(
                jnp.sum(total, axis=-1, keepdims=True), (BLOCK, 128)
            )
        o_ref[:, cols(h)] = dot(
            jnp.concatenate([e_ref[h, n] for n in range(3)], axis=1),
            jnp.concatenate(vs[h], axis=0),
            NN,
        )


def spread(terms, picks, g):
    parts = [t * jnp.where(p == g, 1.0, 0.0).astype(F32) for t, p in zip(terms, picks)]
    return (parts[0] + parts[1]).astype(BF16)


def far_kernel(
    part_ref, qn_ref, cot_ref, x2, x1, y2, y1, o_ref, l_ref, eb_ref, db_ref,
    g2_ref, g1_ref, gb_ref, out_ref, rl_ref, delta_ref, dq_ref, e_ref, d_ref,
):
    scale = 128 ** (-0.5)
    levels = (x2, x1, y2, y1)
    each = [(h, i) for h in range(HEADS) for i in range(2)]
    pick = [[part_ref[i, n] & 1 for n in range(LEVELS)] for i in range(2)]
    q = {(h, i): qn_ref[rows(i), cols(h)] for h, i in each}
    ct = {(h, i): cot_ref[rows(i), cols(h)] for h, i in each}
    ks = {
        (h, i): jnp.concatenate([picked(r, 0, p, h) for r, p in zip(levels, pick[i])], axis=0)
        for h, i in each
    }
    vs = {
        (h, i): jnp.concatenate([picked(r, 1, p, h) for r, p in zip(levels, pick[i])], axis=0)
        for h, i in each
    }
    e = {t: jnp.exp(dot(q[t], ks[t], NT) * scale) for t in each}
    dp = {t: dot(ct[t], vs[t], NT) for t in each}
    low = {t: e[t].astype(BF16) for t in each}
    far_o = {t: dot(low[t], vs[t], NN) for t in each}
    p, ds, rl, delta = {}, {}, {}, {}
    for t in each:
        h, i = t
        total = e[t][:, :128] + e[t][:, 128:256] + e[t][:, 256:384] + e[t][:, 384:]
        total = l_ref[h, rows(i), :1] + jnp.sum(total, axis=-1, keepdims=True)
        rl[t] = 1.0 / total
        o = ((o_ref[rows(i), cols(h)] + far_o[t]) * rl[t]).astype(BF16)
        out_ref[rows(i), cols(h)] = o
        delta[t] = jnp.sum(ct[t].astype(F32) * o.astype(F32), axis=-1, keepdims=True)
        rl_ref[h, rows(i), :] = jnp.broadcast_to(rl[t], (BLOCK, 128))
        delta_ref[h, rows(i), :] = jnp.broadcast_to(delta[t], (BLOCK, 128))
        y = slice(256, 512)
        p[t] = e[t][:, y] * rl[t]
        ds[t] = (p[t] * (dp[t][:, y] - delta[t])).astype(BF16)
    dk = {t: dot(ds[t], q[t], TN) * scale for t in each}
    dv = {t: dot(p[t].astype(BF16), ct[t], TN) for t in each}
    for h in range(HEADS):
        for n, ref in enumerate((g2_ref, g1_ref)):
            picks = [pick[i][2 + n] for i in range(2)]
            for g in range(2):
                ref[0, rows(g), cols(h)] = spread([dk[h, i][rows(n)] for i in range(2)], picks, g)
                ref[1, rows(g), cols(h)] = spread([dv[h, i][rows(n)] for i in range(2)], picks, g)
    for h in range(HEADS):
        full = [jnp.concatenate((v[h, 0], v[h, 1]), axis=0) for v in (rl, delta, q, ct)]
        pb = eb_ref[h, 2].astype(F32) * full[0]
        dsb = (pb * (db_ref[h, 2].astype(F32) - full[1])).astype(BF16)
        gb_ref[0, :, cols(h)] = (dot(dsb, full[2], TN) * scale).astype(BF16)
        gb_ref[1, :, cols(h)] = dot(pb.astype(BF16), full[3], TN).astype(BF16)
    for t in each:
        h, i = t
        dq_ref[rows(i), cols(h)] = dot(ds[t], ks[t][256:], NN)
        for n in range(2):
            e_ref[h, n, rows(i), :] = low[t][:, rows(n)]
            d_ref[h, n, rows(i), :] = dp[t][:, rows(n)].astype(BF16)


def near_kernel(
    part_ref, q_ref, gain_ref, qn_ref, cot_ref, own, mate, zpair, zup, zdown, x2, x1, e_ref, d_ref,
    ex_ref, dx_ref, rl_ref, delta_ref, dqy_ref,
    gx2_ref, gx1_ref, gm_ref, gown_ref, gq_ref,
):
    scale = 128 ** (-0.5)
    pick = [[part_ref[i, n] & 1 for n in range(2)] for i in range(2)]
    for h in range(HEADS):
        qn = qn_ref[:, cols(h)]
        ct = cot_ref[:, cols(h)]
        rl = rl_ref[h]
        delta = delta_ref[h]
        x_grads = []
        for n, ref in enumerate((gx2_ref, gx1_ref)):
            p = ex_ref[h, n].astype(F32) * rl
            w = p.astype(BF16)
            ds = (p * (dx_ref[h, n].astype(F32) - delta)).astype(BF16)
            x_grads.append(ds)
            picks = [pick[i][n] for i in range(2)]
            k_terms = [dot(ds[rows(i)], qn[rows(i)], TN) * scale for i in range(2)]
            v_terms = [dot(w[rows(i)], ct[rows(i)], TN) for i in range(2)]
            for g in range(2):
                ref[0, rows(g), cols(h)] = spread(k_terms, picks, g)
                ref[1, rows(g), cols(h)] = spread(v_terms, picks, g)
        rl2 = jnp.concatenate((rl, rl), axis=1)
        delta2 = jnp.concatenate((delta, delta), axis=1)
        grads = []
        for n, ref in enumerate((gown_ref, gm_ref, None)):
            p = e_ref[h, n].astype(F32) * rl2
            ds = (p * (d_ref[h, n].astype(F32) - delta2)).astype(BF16)
            grads.append(ds)
            if ref is None:
                continue
            ref[0, :, cols(h)] = (dot(ds, qn, TN) * scale).astype(ref.dtype)
            ref[1, :, cols(h)] = dot(p.astype(BF16), ct, TN).astype(ref.dtype)
        normed, inverse, _ = norm(q_ref[:, cols(h)], gain_ref[h : h + 1, :])
        band = dot(
            jnp.concatenate(grads, axis=1),
            jnp.concatenate(near_part(own, mate, zpair, zup, zdown, 0, h), axis=0),
            NN,
        )
        for i in range(2):
            dq = dot(
                jnp.concatenate([g[rows(i)] for g in x_grads], axis=1),
                jnp.concatenate([picked(r, 0, p, h) for r, p in zip((x2, x1), pick[i])], axis=0),
                NN,
            )
            dq = (dq + band[rows(i)] + dqy_ref[rows(i), cols(h)]) * scale
            gq_ref[rows(i), cols(h)] = norm_back(
                dq, normed[rows(i)], inverse[rows(i)], gain_ref[h : h + 1, :]
            ).astype(BF16)


def gather_kernel(own, a, b, c, d, e, f, out_ref):
    total = own[...]
    for t in (a, b, c, d, e, f):
        total = total + t[...].astype(F32)
    out_ref[...] = total


def final_kernel(k_ref, gain_ref, own, a, b, gk_ref, gv_ref):
    terms = (a, b)
    for n in range(HEADS):
        dk = own[0, :, cols(n)]
        dv = own[1, :, cols(n)]
        for t in terms:
            dk = dk + t[0, :, cols(n)].astype(F32)
            dv = dv + t[1, :, cols(n)].astype(F32)
        normed, inverse, _ = norm(k_ref[:, cols(n)], gain_ref[n : n + 1, :])
        gk_ref[:, cols(n)] = norm_back(dk, normed, inverse, gain_ref[n : n + 1, :]).astype(BF16)
        gv_ref[:, cols(n)] = dv.astype(BF16)


V = pl.BlockSpec(memory_space=pltpu.VMEM)
S = pl.BlockSpec(memory_space=pltpu.SMEM)
H = pl.BlockSpec(memory_space=pltpu.HBM)


def call(kernel, specs, outs, flops, *args, scratch=()):
    shapes = [jax.ShapeDtypeStruct(s, t) for s, t in outs]
    moved = sum(a.size * a.dtype.itemsize for a in args)
    moved += sum(s.size * s.dtype.itemsize for s in shapes)
    return pl.pallas_call(
        kernel,
        out_shape=shapes,
        in_specs=specs,
        out_specs=[V] * len(shapes),
        scratch_shapes=scratch,
        compiler_params=pltpu.CompilerParams(vmem_limit_bytes=24 * 2**20),
        cost_estimate=pl.CostEstimate(flops=flops, transcendentals=0, bytes_accessed=moved),
    )(*args)


def body(query_raw, key_raw, values, band_reach, partners, gain_query, gain_key, cotangent):
    count = lax.axis_size(AXES)
    device = lax.axis_index(AXES).astype(jnp.int32).reshape(1)
    mates = [(i, i ^ 1) for i in range(count)]
    run = lax.axis_size("ctx") // 2
    joints = [(a, a + 1) for a in range(1, count - 1, 2)]
    cross_up = [(a, b) for a, b in joints if a // run != b // run]
    cross_down = [(b, a) for a, b in cross_up]
    inner = [(a, b) for a, b in joints if a // run == b // run]
    inner = [p for a, b in inner for p in ((a, b), (b, a))]
    masks = [count >> (level + 1) for level in range(LEVELS)]
    across = [[(i, i ^ m) for i in range(count)] for m in masks]

    def send(value, perm):
        return lax.ppermute(value, AXES, perm)

    pack_t = ((2, 256, 256), BF16)

    (pack,) = call(
        prep_kernel, [H, H, H], [pack_t], 10**6,
        *[pltpu.with_memory_space_constraint(a, pltpu.HBM) for a in (key_raw, values, gain_key)],
        scratch=[
            pltpu.VMEM((256, 256), BF16), pltpu.VMEM((HEADS, 128), F32),
            pltpu.SemaphoreType.DMA((3,)),
        ],
    )
    y2 = send(pack, across[2])
    y1 = send(pack, across[3])
    x2 = send(pack, across[0])
    x1 = send(pack, across[1])
    mate = send(pack, mates)
    zpair = send(pack, inner)
    zup = send(pack, cross_up)
    zdown = send(pack, cross_down)

    tiles = ((HEADS, 3, 256, 256), BF16)
    x_tiles = ((HEADS, 2, 256, 128), BF16)
    rowstat = ((HEADS, 256, 128), F32)
    full = ((256, 256), F32)
    qn, e, d, o_part, l_part = call(
        functools.partial(local_kernel, last_block=2 * count - 1),
        [S, S, S] + [V] * 8,
        [((256, 256), BF16), tiles, tiles, full, rowstat],
        20 * 3 * 2 * 128**3,
        device, band_reach, partners, query_raw, gain_query, cotangent, pack, mate, zpair, zup, zdown,
    )
    gy2, gy1, gb, out, rl, delta, dqy, ex, dx = call(
        far_kernel,
        [S] + [V] * 10,
        [pack_t, pack_t, pack_t, ((256, 256), BF16), rowstat, rowstat, full, x_tiles, x_tiles],
        8 * 9 * 2 * 128**3,
        partners, qn, cotangent, x2, x1, y2, y1, o_part, l_part, e, d,
    )
    ry2 = send(gy2, across[2])
    ry1 = send(gy1, across[3])
    gx2, gx1, gm, gown, grad_query = call(
        near_kernel,
        [S] + [V] * 18,
        [pack_t, pack_t, pack_t, ((2, 256, 256), F32), ((256, 256), BF16)],
        28 * 3 * 2 * 128**3,
        partners, query_raw, gain_query, qn, cotangent, pack, mate, zpair, zup, zdown, x2, x1, e, d,
        ex, dx, rl, delta, dqy,
    )
    rx2 = send(gx2, across[0])
    rx1 = send(gx1, across[1])
    rm = send(gm, mates)
    rb = send(gb, inner)
    ru = send(gb, cross_up)
    rd = send(gb, cross_down)
    (gsum,) = call(
        gather_kernel, [V] * 7, [((2, 256, 256), F32)], 10**6,
        gown, ry2, ry1, rx2, rx1, rb, ru,
    )
    grad_key, grad_value = call(
        final_kernel,
        [V] * 5,
        [((256, 256), BF16), ((256, 256), BF16)],
        10**6,
        key_raw, gain_key, gsum, rm, rd,
    )
    return (out, grad_query, grad_key, grad_value)


def solution(mesh):
    wide = P(AXES, None)
    return jax.shard_map(
        body,
        mesh=mesh,
        in_specs=(wide, wide, wide, P(AXES), wide, P(), P(), wide),
        out_specs=(wide, wide, wide, wide),
        check_vma=False,
    )
```
